256 devices in a mesh: row: 16 (over x, z_hi), col: 16 (over y, z_lo, core).
Axes of the slice: x: 4, y: 4, z: 8 (z_hi: 4, z_lo: 2; z = z_hi * 2 + z_lo), core: 2. Of those that a mesh axis runs over, the one named last changes fastest.
Arguments:
- object_field: float32 [2, 6144, 6144], P(None, 'row', 'col'), may hold values from -6 to 6
- probe: float32 [2, 256, 256], replicated, may hold values from -5 to 5
- amplitudes: float32 [8192, 8192], P('row', 'col'), may hold values from 0.2 to 3
- offsets: int32 [32, 32, 2], P('row', 'col'), may hold values from 0 to 128, as said below
Outputs:
- updated_object: float32 [2, 6144, 6144], P(None, 'row', 'col')
The draws below stay inside these ranges and needn't reach their ends.
Inputs may be any that keep to these rules, and one draw needn't show every extreme that they name: Both offsets of every scan position lie in 0 to 128, and each end of that range is taken in every draw.
All inputs are finite; a program needn't handle non-finite values.
Results may differ from the reference program's by a relative error of at most 0.0003.
Values sent between devices are 32-bit elements; how exact they have to be, the bound alone decides.
A program may use at most 64 MiB of HBM per device.

```python
import math
import jax
import jax.numpy as jnp
from jax import lax

TILE = 384
WIN = 256
MARGIN = 96
ITERS = 2
PITCH = 192
SCAN_ROWS = 32
SCAN_COLS = 32
OBJ_ROWS = 6144
OBJ_COLS = 6144
AMP_ROWS = 8192
AMP_COLS = 8192


def draw_offsets(key, part):
    top = 2 * MARGIN + TILE - PITCH - WIN
    values = jax.random.randint(key, (SCAN_ROWS, SCAN_COLS, 2), 0, top + 1)
    values = values.at[0, 0, 0].set(0).at[0, 0, 1].set(top)
    values = values.at[SCAN_ROWS - 1, SCAN_COLS - 1, 0].set(top).at[SCAN_ROWS - 1, SCAN_COLS - 1, 1].set(0)
    return values.astype(jnp.int32)


def level_of(stream_key, dims, pieces, smallest, high):
    gain, own = 1.0, jax.random.fold_in(stream_key, 6)
    for axis_at, blocks in pieces:
        draws = jnp.exp(jax.random.uniform(jax.random.fold_in(own, axis_at), (blocks,), jnp.float32, smallest / len(pieces), high / len(pieces)))
        gain = gain * jnp.repeat(draws, dims[axis_at] // blocks).reshape([-1 if axis == axis_at else 1 for axis in range(len(dims))])
    return gain


def normal_values(own_key, extent, deviation, reach, shards=(), held_as=jnp.bfloat16):
    result = deviation * jax.random.normal(own_key, extent, jnp.float32)
    if shards:
        result = result * level_of(own_key, extent, shards, -0.22, 0.18)
    return jnp.clip(result, -reach, reach).astype(held_as)


def setup_inputs(seed: int = 0) -> dict:
    arg_keys = jax.random.split(jax.random.key(seed), 5)
    object_field = normal_values(arg_keys[0], (2, OBJ_ROWS, OBJ_COLS), 1.0, 6.0, ((1, 16), (2, 16)), jnp.float32)
    probe = normal_values(arg_keys[1], (2, WIN, WIN), 0.7, 5.0, (), jnp.float32)
    amplitudes = jnp.clip(jnp.exp(math.log(3.0) - 2.7080502 * jax.random.uniform(arg_keys[2], (AMP_ROWS, AMP_COLS), jnp.float32) ** level_of(arg_keys[2], (AMP_ROWS, AMP_COLS), ((0, 16), (1, 16)), -0.2, 0.2)), 0.2, 3.0)
    offsets = draw_offsets(jax.random.fold_in(arg_keys[4], 71), 0)
    return {"object_field": object_field, "probe": probe, "amplitudes": amplitudes, "offsets": offsets}


step_size = 0.3
tv_weight = 0.2
tv_smooth = 0.1
amp_floor = 0.5

def tv_from_extended(extended):
    base = extended[:, :-1, :-1]
    diff_down = extended[:, 1:, :-1] - base
    diff_right = extended[:, :-1, 1:] - base
    scale = jnp.sqrt(lax.optimization_barrier(jnp.sum(diff_down * diff_down + diff_right * diff_right, axis=0)) + tv_smooth)
    flow_down = diff_down / scale
    flow_right = diff_right / scale
    return flow_down[:, :-1, 1:] - flow_down[:, 1:, 1:] + flow_right[:, 1:, :-1] - flow_right[:, 1:, 1:]

def window_gradient(window, probe, amp):
    probe_c = probe[0] + 1j * probe[1]
    field = probe_c * (window[0] + 1j * window[1])
    spectrum = jnp.fft.fft2(field, norm='ortho')
    magnitude = jnp.abs(spectrum)
    misfit = spectrum * (1.0 - amp / jnp.maximum(magnitude, amp_floor))
    back = jnp.fft.ifft2(misfit, norm='ortho')
    grad = jnp.conj(probe_c) * back
    return jnp.stack([jnp.real(grad), jnp.imag(grad)])

def reference(object_field, probe, amplitudes, offsets):
    amp_tiles = amplitudes.reshape(SCAN_ROWS, WIN, SCAN_COLS, WIN).transpose(0, 2, 1, 3).reshape(-1, WIN, WIN)
    offset_list = offsets.reshape(-1, 2)
    numbers = jnp.arange(SCAN_ROWS * SCAN_COLS, dtype=jnp.int32)
    obj = object_field
    zero = jnp.int32(0)
    for step in range(ITERS):
        padded = jnp.pad(obj, ((0, 0), (MARGIN, MARGIN), (MARGIN, MARGIN)))

        def visit(canvas, item):
            number, offset, amp = item
            start_row = (number // SCAN_COLS * PITCH + offset[0]).astype(jnp.int32)
            start_col = (number % SCAN_COLS * PITCH + offset[1]).astype(jnp.int32)
            window = lax.dynamic_slice(padded, (zero, start_row, start_col), (2, WIN, WIN))
            grad = window_gradient(window, probe, amp)
            piece = lax.dynamic_slice(canvas, (zero, start_row, start_col), (2, WIN, WIN))
            canvas = lax.dynamic_update_slice(canvas, piece + grad, (zero, start_row, start_col))
            return (canvas, None)
        canvas, _ = lax.scan(visit, jnp.zeros_like(padded), (numbers, offset_list, amp_tiles))
        grad = canvas[:, MARGIN:MARGIN + OBJ_ROWS, MARGIN:MARGIN + OBJ_COLS]
        edged = jnp.pad(obj, ((0, 0), (1, 1), (1, 1)))
        obj = obj - step_size * (grad + tv_weight * tv_from_extended(edged))
    return obj
```

```python
import functools

import jax
import jax.numpy as jnp
import ml_dtypes
import numpy as np
from jax import lax
from jax.experimental import pallas as pl
from jax.experimental.pallas import tpu as pltpu
from jax.sharding import PartitionSpec as P

WIN = 256
HALF = 128
MARGIN = 96
PITCH = 192
TILE = 384
ROWS = TILE + 2 * MARGIN
COLS = 640
OWN = 128

step_size = 0.3
tv_weight = 0.2
tv_smooth = 0.1
amp_floor = 0.5

MESH = pl.DeviceIdType.MESH


def dft_tables():
    n = np.arange(HALF)
    whole = []
    for odd in (0, 1):
        k = 2 * np.arange(HALF) + odd
        angle = 2.0 * np.pi * ((k[:, None] * n[None, :]) % WIN) / WIN
        cosine = np.cos(angle) / 16.0
        sine = np.sin(angle) / 16.0
        left_form = np.block([[cosine, sine], [-sine, cosine]])
        whole += [left_form, left_form.T]
    high = [m.astype(ml_dtypes.bfloat16) for m in whole]
    low = [(m - h.astype(np.float64)).astype(ml_dtypes.bfloat16) for m, h in zip(whole, high)]
    return np.stack(high + low)


def parity_table():
    table = np.zeros((WIN, WIN), ml_dtypes.bfloat16)
    order = np.concatenate([np.arange(0, WIN, 2), np.arange(1, WIN, 2)])
    table[order, np.arange(WIN)] = 1.0
    return np.stack([table, table.T])


def split(x):
    high = x.astype(jnp.bfloat16)
    return high, (x - high.astype(jnp.float32)).astype(jnp.bfloat16)


def thirds(x):
    high = x.astype(jnp.bfloat16)
    return high, *split(x - high.astype(jnp.float32))


def dot(a, b):
    return jnp.dot(a, b, preferred_element_type=jnp.float32)


def cat(a, b, axis):
    return jnp.concatenate([a, b], axis=axis)


def left(tables, k, x):
    high, low = split(x)
    return dot(tables[k], high) + dot(tables[k], low) + dot(tables[k + 4], high)


def right(x, tables, k):
    high, low = split(x)
    return dot(high, tables[k]) + dot(low, tables[k]) + dot(high, tables[k + 4])


def fitted(spectrum, amp):
    re, im = spectrum[:, :HALF], spectrum[:, HALF:]
    magnitude = jnp.sqrt(re * re + im * im)
    keeping = 1.0 - amp / jnp.maximum(magnitude, amp_floor)
    return cat(re * keeping, im * keeping, 1)


def back_field(re, im, amp, tables):
    even = left(tables, 0, cat(re[:HALF] + re[HALF:], im[:HALF] + im[HALF:], 0))
    odd = left(tables, 2, cat(re[:HALF] - re[HALF:], im[:HALF] - im[HALF:], 0))
    re, im = cat(even[:HALF], odd[:HALF], 0), cat(even[HALF:], odd[HALF:], 0)
    even = cat(re[:, :HALF] + re[:, HALF:], im[:, :HALF] + im[:, HALF:], 1)
    odd = cat(re[:, :HALF] - re[:, HALF:], im[:, :HALF] - im[:, HALF:], 1)
    even = fitted(right(even, tables, 1), amp[:, :HALF])
    odd = fitted(right(odd, tables, 3), amp[:, HALF:])
    u, v = right(even, tables, 0), right(odd, tables, 2)
    p, m = u + v, u - v
    re, im = cat(p[:, :HALF], m[:, :HALF], 1), cat(p[:, HALF:], m[:, HALF:], 1)
    u = left(tables, 1, cat(re[:HALF], im[:HALF], 0))
    v = left(tables, 3, cat(re[HALF:], im[HALF:], 0))
    p, m = u + v, u - v
    return cat(p[:HALF], m[:HALF], 0), cat(p[HALF:], m[HALF:], 0)


def window(ext, canvas, probes, amps, tables, row_shift, col_shift, number):
    top, first = number // 2 * PITCH, number % 2 * HALF
    by_row = lax.broadcasted_iota(jnp.int32, (HALF, WIN), 0) >= row_shift
    by_col = lax.broadcasted_iota(jnp.int32, (HALF, WIN), 1) >= col_shift

    def rows_at(part, start):
        near = ext[part, start : start + HALF, first : first + WIN]
        far = ext[part, start : start + HALF, first + WIN : first + 2 * WIN]
        return jnp.where(by_col, near, far)

    def cells(part):
        upper = jnp.where(by_row, rows_at(part, top), rows_at(part, top + WIN))
        return cat(upper, rows_at(part, top + HALF), 0)

    re, im = cells(0), cells(1)
    probe_re, probe_im = probes[number, 0], probes[number, 1]
    back_re, back_im = back_field(
        probe_re * re - probe_im * im, probe_re * im + probe_im * re, amps[number], tables
    )
    grads = (probe_re * back_re + probe_im * back_im, probe_re * back_im - probe_im * back_re)
    for part, grad in enumerate(grads):
        upper, lower = grad[:HALF], grad[HALF:]
        for start, value in (
            (top, jnp.where(by_row, upper, 0.0)),
            (top + HALF, lower),
            (top + WIN, jnp.where(by_row, 0.0, upper)),
        ):
            canvas[part, start : start + HALF, first : first + WIN] += jnp.where(by_col, value, 0.0)
            canvas[part, start : start + HALF, first + WIN : first + 2 * WIN] += jnp.where(
                by_col, 0.0, value
            )


def rolled(x, shift, axis):
    amount = jnp.full(x.shape, shift, jnp.int32)
    for bit in range(8):
        x = jnp.where((amount & (1 << bit)) != 0, pltpu.roll(x, 1 << bit, axis), x)
    return x


def lane_part(depth):
    return lax.broadcasted_iota(jnp.int32, (depth, 128), 1) // 32


def turned(x, amount):
    amount %= 128
    return pltpu.roll(x, amount, 1) if amount else x


def pack(source, lane, skip, starts, depth, target):
    part_of = lane_part(depth)
    for part in range(2):
        groups = [source[part, s : s + depth, lane : lane + 128] for s in starts]
        for third in range(3):
            value = turned(groups[0], -32 * third - skip)
            for g in range(1, 4):
                value = jnp.where(part_of == g, turned(groups[g], 32 * (g - third) - skip), value)
            target[part, third * depth : (third + 1) * depth, :] = value


def unpack(source, skip, depth, part, g, keep):
    part_of = lane_part(depth)
    value = jnp.zeros((depth, 128), jnp.float32)
    for third in range(3):
        block = turned(source[part, third * depth : (third + 1) * depth, :], skip + 32 * (third - g))
        value = jnp.where(part_of == third + skip // 32, block, value)
    return jnp.where(keep, value, 0.0)


def tv_rows(ext, start, depth):
    high = depth + 16
    first = MARGIN + start - 8
    fields = [ext[part, pl.ds(first, high), :] for part in range(2)]
    down = [pltpu.roll(f, high - 1, 0) - f for f in fields]
    right_ = [pltpu.roll(f, COLS - 1, 1) - f for f in fields]
    total = down[0] * down[0] + right_[0] * right_[0] + (down[1] * down[1] + right_[1] * right_[1])
    inverse = lax.rsqrt(total + tv_smooth)
    out = []
    for part in range(2):
        flow_down = down[part] * inverse
        flow_right = right_[part] * inverse
        value = pltpu.roll(flow_down, 1, 0) - flow_down + pltpu.roll(flow_right, 1, 1) - flow_right
        out.append(value[8 : depth + 8, OWN : OWN + TILE])
    return out


BLOCKS = (slice(OWN, OWN + 128), slice(OWN + 128, OWN + 256), slice(OWN + 256, OWN + 384))
EDGE_ROWS = ((0, 96, 384, 480), 96)
MID_ROWS = ((192, 240, 288, 336), 48)
OWN_ROWS = ((96, 192, 288, 384), 96)
CORNER_ROWS = ((0, 48, 480, 528), 48)


def kernel(
    offsets, obj, probe, amplitudes, tables, parity, out,
    ext, canvas, probes, amps,
    own_send, own_recv, corner_send, corner_recv,
    grad_edge_send, grad_edge_recv, grad_mid_send, grad_mid_recv,
    rows_recv,
    halo_mid_send, halo_mid_recv, halo_edge_send, halo_edge_recv,
    last_edge_send, last_edge_recv, last_mid_send, last_mid_recv,
    last_rows_recv,
    send_sem, recv_sem,
):
    row, col = lax.axis_index("row"), lax.axis_index("col")
    rows, cols = lax.axis_size("row"), lax.axis_size("col")
    above, below = (lax.rem(row + rows - 1, rows), col), (lax.rem(row + 1, rows), col)
    before, after = (row, lax.rem(col + cols - 1, cols)), (row, lax.rem(col + 1, cols))
    has_above, has_below = row > 0, row < rows - 1
    has_before, has_after = col > 0, col < cols - 1

    barrier = pltpu.get_barrier_semaphore()
    for device in (above, below, before, after):
        pl.semaphore_signal(barrier, inc=1, device_id=device, device_id_type=MESH)
    pl.semaphore_wait(barrier, 4)

    count = [0]
    everything, waited = [], []

    def send(source, target, device):
        number = count[0]
        count[0] += 1
        copy = pltpu.make_async_remote_copy(
            src_ref=source, dst_ref=target, send_sem=send_sem.at[number], recv_sem=recv_sem.at[number],
            device_id=device, device_id_type=MESH,
        )
        copy.start()
        everything.append(copy)
        return copy

    def send_rows(source, target, low, high, low_to, high_to, depth, source_lane, target_lane, block):
        a = slice(source_lane + 128 * block, source_lane + 128 * block + 128)
        b = slice(target_lane + 128 * block, target_lane + 128 * block + 128)
        return [
            send(source.at[:, low : low + depth, a], target(0).at[:, low_to : low_to + depth, b], above),
            send(source.at[:, high : high + depth, a], target(1).at[:, high_to : high_to + depth, b], below),
        ]

    def send_cols(source, lanes, groups, depth, sends, recvs):
        pack(source, lanes[0][0], lanes[0][1], groups, depth, sends.at[0])
        first = send(sends.at[0], recvs.at[0], before)
        pack(source, lanes[1][0], lanes[1][1], groups, depth, sends.at[1])
        return [first, send(sends.at[1], recvs.at[1], after)]

    def arrived(copies):
        for copy in copies:
            copy.wait_recv()

    own_lanes = ((OWN, 0), (OWN + 256, 32))
    margin_lanes = ((0, 32), (OWN + TILE, 0))

    first_rows = [
        send_rows(obj, lambda _: ext, 0, TILE - MARGIN, MARGIN + TILE, 0, MARGIN, 0, OWN, block)
        for block in (0, 2)
    ]
    ext[:, MARGIN : MARGIN + TILE, OWN : OWN + TILE] = obj[...]
    first_cols = send_cols(ext, own_lanes, *OWN_ROWS, own_send, own_recv)
    first_rows.append(
        send_rows(obj, lambda _: ext, 0, TILE - MARGIN, MARGIN + TILE, 0, MARGIN, 0, OWN, 1)
    )

    shifts = []
    for number in range(4):
        i, j = number // 2, number % 2
        shifts.append((offsets[i, j, 0], offsets[i, j, 1] + 32 + 64 * j))
    for number in range(4):
        for part in range(2):
            probes[number, part] = rolled(
                rolled(probe[part], shifts[number][0], 0), shifts[number][1], 1
            )
        i, j = number // 2, number % 2
        pattern = amplitudes[i * WIN : (i + 1) * WIN, j * WIN : (j + 1) * WIN]
        pattern = sum(dot(piece, parity[0]) for piece in thirds(pattern))
        amps[number] = sum(dot(parity[1], piece) for piece in thirds(pattern))
    canvas[...] = jnp.zeros_like(canvas)

    def settle_rows(block):
        arrived(first_rows[(0, 2, 1)[block]])
        lanes = BLOCKS[block]
        for start, keep in ((0, has_above), (MARGIN + TILE, has_below)):
            halo = ext[:, start : start + MARGIN, lanes]
            ext[:, start : start + MARGIN, lanes] = jnp.where(keep, halo, 0.0)

    settle_rows(0)
    settle_rows(2)
    first_corners = send_cols(ext, own_lanes, *CORNER_ROWS, corner_send, corner_recv)
    settle_rows(1)

    def place_halo(recvs, groups, depth):
        for part in range(2):
            for g, start in enumerate(groups):
                ext[part, start : start + depth, OWN + TILE :] = unpack(
                    recvs.at[0], 0, depth, part, g, has_after
                )
                ext[part, start : start + depth, :OWN] = unpack(
                    recvs.at[1], 32, depth, part, g, has_before
                )

    arrived(first_cols)
    place_halo(own_recv, *OWN_ROWS)
    arrived(first_corners)
    place_halo(corner_recv, *CORNER_ROWS)

    def gradients():
        for number in range(4):
            window(ext, canvas, probes, amps, tables, *shifts[number], number)

    def add_cols(recvs, groups, depth):
        for part in range(2):
            for g, start in enumerate(groups):
                canvas[part, start : start + depth, BLOCKS[2]] += unpack(
                    recvs.at[0], 32, depth, part, g, has_after
                )
                canvas[part, start : start + depth, BLOCKS[0]] += unpack(
                    recvs.at[1], 0, depth, part, g, has_before
                )

    gradients()
    edge_cols = send_cols(canvas, margin_lanes, *EDGE_ROWS, grad_edge_send, grad_edge_recv)
    mid_cols = send_cols(canvas, margin_lanes, *MID_ROWS, grad_mid_send, grad_mid_recv)

    def add_tv(number, carry):
        start = pl.multiple_of(number * 48, 8)
        for part, value in enumerate(tv_rows(ext, start, 48)):
            canvas[part, pl.ds(MARGIN + start, 48), OWN : OWN + TILE] += tv_weight * value
        return carry

    lax.fori_loop(0, 8, add_tv, 0)

    def send_middle(block):
        return send_rows(
            canvas, lambda k: rows_recv.at[k], 0, 384, 0, 0, 192, OWN, 0, block
        )

    def taken_rows(block):
        lanes = BLOCKS[block]
        theirs = slice(128 * block, 128 * block + 128)
        for start, source, keep, halo in ((384, 0, has_below, 480), (0, 1, has_above, 0)):
            inner = 384 if start else 96
            for part in range(2):
                for first, gate in ((halo, None), (inner, keep)):
                    at = first - start
                    theirs_sum = jnp.where(keep, rows_recv[source, part, at : at + 96, theirs], 0.0)
                    total = canvas[part, first : first + 96, lanes] + theirs_sum
                    if gate is None:
                        total = jnp.where(keep, total, 0.0)
                    ext[part, first : first + 96, lanes] -= step_size * total

    row_sums = {1: send_middle(1)}
    arrived(edge_cols)
    add_cols(grad_edge_recv, *EDGE_ROWS)
    row_sums[0] = send_middle(0)
    row_sums[2] = send_middle(2)
    arrived(mid_cols)
    add_cols(grad_mid_recv, *MID_ROWS)
    ext[:, 192:384, OWN : OWN + TILE] -= step_size * canvas[:, 192:384, OWN : OWN + TILE]
    mid_halo = send_cols(ext, own_lanes, *MID_ROWS, halo_mid_send, halo_mid_recv)
    for block in (0, 2):
        arrived(row_sums[block])
        taken_rows(block)
    edge_halo = send_cols(ext, own_lanes, *EDGE_ROWS, halo_edge_send, halo_edge_recv)
    arrived(row_sums[1])
    taken_rows(1)
    for copies in (edge_cols, mid_cols, *row_sums.values()):
        for copy in copies:
            copy.wait_send()
            waited.append(copy)
    canvas[...] = jnp.zeros_like(canvas)
    arrived(mid_halo)
    place_halo(halo_mid_recv, *MID_ROWS)
    arrived(edge_halo)
    place_halo(halo_edge_recv, *EDGE_ROWS)

    gradients()

    def send_last(block):
        return send_rows(
            canvas, lambda k: last_rows_recv.at[k], 0, MARGIN + TILE, 0, 0, MARGIN, OWN, 0, block
        )

    edge_cols = send_cols(canvas, margin_lanes, *EDGE_ROWS, last_edge_send, last_edge_recv)
    mid_cols = send_cols(canvas, margin_lanes, *MID_ROWS, last_mid_send, last_mid_recv)
    last_rows = {1: send_last(1)}

    def start_out(number, carry):
        start = pl.multiple_of(number * 48, 8)
        here = pl.ds(MARGIN + start, 48)
        for part, value in enumerate(tv_rows(ext, start, 48)):
            out[part, pl.ds(start, 48), :] = (
                ext[part, here, OWN : OWN + TILE] - (step_size * tv_weight) * value
            )
        return carry

    lax.fori_loop(0, 8, start_out, 0)
    arrived(edge_cols)
    add_cols(last_edge_recv, *EDGE_ROWS)
    last_rows[0] = send_last(0)
    last_rows[2] = send_last(2)
    arrived(mid_cols)
    add_cols(last_mid_recv, *MID_ROWS)
    out[...] -= step_size * canvas[:, MARGIN : MARGIN + TILE, OWN : OWN + TILE]
    for block in (1, 0, 2):
        arrived(last_rows[block])
        lanes = slice(128 * block, 128 * block + 128)
        for start, source, keep in ((TILE - MARGIN, 0, has_below), (0, 1, has_above)):
            theirs = jnp.where(keep, last_rows_recv[source, :, :, lanes], 0.0)
            out[:, start : start + MARGIN, lanes] -= step_size * theirs
    for copy in everything:
        if not any(copy is other for other in waited):
            copy.wait_send()


def on_device(object_field, probe, amplitudes, offsets):
    vmem = pl.BlockSpec(memory_space=pltpu.VMEM)

    def pair(depth):
        return [pltpu.VMEM((2, 2, depth, 128), jnp.float32)] * 2

    return pl.pallas_call(
        kernel,
        out_shape=jax.ShapeDtypeStruct((2, TILE, TILE), jnp.float32),
        in_specs=[pl.BlockSpec(memory_space=pltpu.SMEM)] + [vmem] * 5,
        out_specs=vmem,
        scratch_shapes=[
            pltpu.VMEM((2, ROWS, COLS), jnp.float32),
            pltpu.VMEM((2, ROWS, COLS), jnp.float32),
            pltpu.VMEM((4, 2, WIN, WIN), jnp.float32),
            pltpu.VMEM((4, WIN, WIN), jnp.float32),
            *pair(288), *pair(144),
            *pair(288), *pair(144),
            pltpu.VMEM((2, 2, 192, TILE), jnp.float32),
            *pair(144), *pair(288),
            *pair(288), *pair(144),
            pltpu.VMEM((2, 2, MARGIN, TILE), jnp.float32),
            pltpu.SemaphoreType.DMA((34,)),
            pltpu.SemaphoreType.DMA((34,)),
        ],
        compiler_params=pltpu.CompilerParams(
            collective_id=0, has_side_effects=True, vmem_limit_bytes=56 << 20
        ),
        name="ptycho",
    )(offsets, object_field, probe, amplitudes, jnp.asarray(dft_tables()), jnp.asarray(parity_table()))


def solution(mesh):
    in_specs = (P(None, "row", "col"), P(), P("row", "col"), P("row", "col", None))
    out_specs = P(None, "row", "col")
    return jax.shard_map(
        on_device, mesh=mesh, in_specs=in_specs, out_specs=out_specs, check_vma=False
    )
```

```python
import functools

import jax
import jax.numpy as jnp
import ml_dtypes
import numpy as np
from jax import lax
from jax.experimental import pallas as pl
from jax.experimental.pallas import tpu as pltpu
from jax.sharding import PartitionSpec as P

WIN = 256
HALF = 128
MARGIN = 96
PITCH = 192
TILE = 384
ROWS = TILE + 2 * MARGIN
COLS = 640
OWN = 128

step_size = 0.3
tv_weight = 0.2
tv_smooth = 0.1
amp_floor = 0.5

MESH = pl.DeviceIdType.MESH


def dft_tables():
    n = np.arange(HALF)
    whole = []
    for odd in (0, 1):
        k = 2 * np.arange(HALF) + odd
        angle = 2.0 * np.pi * ((k[:, None] * n[None, :]) % WIN) / WIN
        cosine = np.cos(angle) / 16.0
        sine = np.sin(angle) / 16.0
        left_form = np.block([[cosine, sine], [-sine, cosine]])
        whole += [left_form, left_form.T]
    high = [m.astype(ml_dtypes.bfloat16) for m in whole]
    low = [(m - h.astype(np.float64)).astype(ml_dtypes.bfloat16) for m, h in zip(whole, high)]
    return np.stack(high + low)


def parity_table():
    table = np.zeros((WIN, WIN), ml_dtypes.bfloat16)
    order = np.concatenate([np.arange(0, WIN, 2), np.arange(1, WIN, 2)])
    table[order, np.arange(WIN)] = 1.0
    return np.stack([table, table.T])


def split(x):
    high = x.astype(jnp.bfloat16)
    return high, (x - high.astype(jnp.float32)).astype(jnp.bfloat16)


def thirds(x):
    high = x.astype(jnp.bfloat16)
    return high, *split(x - high.astype(jnp.float32))


def dot(a, b):
    return jnp.dot(a, b, preferred_element_type=jnp.float32)


def cat(a, b, axis):
    return jnp.concatenate([a, b], axis=axis)


def left(tables, k, x):
    high, low = split(x)
    return dot(tables[k], high) + dot(tables[k], low) + dot(tables[k + 4], high)


def right(x, tables, k):
    high, low = split(x)
    return dot(high, tables[k]) + dot(low, tables[k]) + dot(high, tables[k + 4])


def fitted(spectrum, amp):
    re, im = spectrum[:, :HALF], spectrum[:, HALF:]
    magnitude = jnp.sqrt(re * re + im * im)
    keeping = 1.0 - amp / jnp.maximum(magnitude, amp_floor)
    return cat(re * keeping, im * keeping, 1)


def back_field(re, im, amp, tables):
    even = left(tables, 0, cat(re[:HALF] + re[HALF:], im[:HALF] + im[HALF:], 0))
    odd = left(tables, 2, cat(re[:HALF] - re[HALF:], im[:HALF] - im[HALF:], 0))
    re, im = cat(even[:HALF], odd[:HALF], 0), cat(even[HALF:], odd[HALF:], 0)
    even = cat(re[:, :HALF] + re[:, HALF:], im[:, :HALF] + im[:, HALF:], 1)
    odd = cat(re[:, :HALF] - re[:, HALF:], im[:, :HALF] - im[:, HALF:], 1)
    even = fitted(right(even, tables, 1), amp[:, :HALF])
    odd = fitted(right(odd, tables, 3), amp[:, HALF:])
    u, v = right(even, tables, 0), right(odd, tables, 2)
    p, m = u + v, u - v
    re, im = cat(p[:, :HALF], m[:, :HALF], 1), cat(p[:, HALF:], m[:, HALF:], 1)
    u = left(tables, 1, cat(re[:HALF], im[:HALF], 0))
    v = left(tables, 3, cat(re[HALF:], im[HALF:], 0))
    p, m = u + v, u - v
    return cat(p[:HALF], m[:HALF], 0), cat(p[HALF:], m[HALF:], 0)


def window(ext, canvas, probes, amps, tables, row_shift, col_shift, number):
    top, first = number // 2 * PITCH, number % 2 * HALF
    by_row = lax.broadcasted_iota(jnp.int32, (HALF, WIN), 0) >= row_shift
    by_col = lax.broadcasted_iota(jnp.int32, (HALF, WIN), 1) >= col_shift

    def rows_at(part, start):
        near = ext[part, start : start + HALF, first : first + WIN]
        far = ext[part, start : start + HALF, first + WIN : first + 2 * WIN]
        return jnp.where(by_col, near, far)

    def cells(part):
        upper = jnp.where(by_row, rows_at(part, top), rows_at(part, top + WIN))
        return cat(upper, rows_at(part, top + HALF), 0)

    re, im = cells(0), cells(1)
    probe_re, probe_im = probes[number, 0], probes[number, 1]
    back_re, back_im = back_field(
        probe_re * re - probe_im * im, probe_re * im + probe_im * re, amps[number], tables
    )
    grads = (probe_re * back_re + probe_im * back_im, probe_re * back_im - probe_im * back_re)
    for part, grad in enumerate(grads):
        upper, lower = grad[:HALF], grad[HALF:]
        for start, value in (
            (top, jnp.where(by_row, upper, 0.0)),
            (top + HALF, lower),
            (top + WIN, jnp.where(by_row, 0.0, upper)),
        ):
            canvas[part, start : start + HALF, first : first + WIN] += jnp.where(by_col, value, 0.0)
            canvas[part, start : start + HALF, first + WIN : first + 2 * WIN] += jnp.where(
                by_col, 0.0, value
            )


def rolled(x, shift, axis):
    amount = jnp.full(x.shape, shift, jnp.int32)
    for bit in range(8):
        x = jnp.where((amount & (1 << bit)) != 0, pltpu.roll(x, 1 << bit, axis), x)
    return x


def lane_part(depth):
    return lax.broadcasted_iota(jnp.int32, (depth, 128), 1) // 32


def turned(x, amount):
    amount %= 128
    return pltpu.roll(x, amount, 1) if amount else x


def pack(source, lane, skip, starts, depth, target):
    part_of = lane_part(depth)
    for part in range(2):
        groups = [source[part, s : s + depth, lane : lane + 128] for s in starts]
        for third in range(3):
            value = turned(groups[0], -32 * third - skip)
            for g in range(1, 4):
                value = jnp.where(part_of == g, turned(groups[g], 32 * (g - third) - skip), value)
            target[part, third * depth : (third + 1) * depth, :] = value


def unpack(source, skip, depth, part, g, keep):
    part_of = lane_part(depth)
    value = jnp.zeros((depth, 128), jnp.float32)
    for third in range(3):
        block = turned(source[part, third * depth : (third + 1) * depth, :], skip + 32 * (third - g))
        value = jnp.where(part_of == third + skip // 32, block, value)
    return jnp.where(keep, value, 0.0)


def tv_rows(ext, start, depth):
    high = depth + 16
    first = MARGIN + start - 8
    fields = [ext[part, pl.ds(first, high), :] for part in range(2)]
    down = [pltpu.roll(f, high - 1, 0) - f for f in fields]
    right_ = [pltpu.roll(f, COLS - 1, 1) - f for f in fields]
    total = down[0] * down[0] + right_[0] * right_[0] + (down[1] * down[1] + right_[1] * right_[1])
    inverse = lax.rsqrt(total + tv_smooth)
    out = []
    for part in range(2):
        flow_down = down[part] * inverse
        flow_right = right_[part] * inverse
        value = pltpu.roll(flow_down, 1, 0) - flow_down + pltpu.roll(flow_right, 1, 1) - flow_right
        out.append(value[8 : depth + 8, OWN : OWN + TILE])
    return out


BLOCKS = (slice(OWN, OWN + 128), slice(OWN + 128, OWN + 256), slice(OWN + 256, OWN + 384))
EDGE_ROWS = ((0, 96, 384, 480), 96)
MID_ROWS = ((192, 240, 288, 336), 48)
OWN_ROWS = ((96, 192, 288, 384), 96)
CORNER_ROWS = ((0, 48, 480, 528), 48)


def kernel(
    offsets, obj, probe, amplitudes, tables, parity, out,
    ext, canvas, probes, amps,
    own_send, own_recv, corner_send, corner_recv,
    grad_edge_send, grad_edge_recv, grad_mid_send, grad_mid_recv,
    rows_recv,
    halo_mid_send, halo_mid_recv, halo_edge_send, halo_edge_recv,
    last_edge_send, last_edge_recv, last_mid_send, last_mid_recv,
    last_rows_recv,
    send_sem, recv_sem,
):
    row, col = lax.axis_index("row"), lax.axis_index("col")
    rows, cols = lax.axis_size("row"), lax.axis_size("col")
    above, below = (lax.rem(row + rows - 1, rows), col), (lax.rem(row + 1, rows), col)
    before, after = (row, lax.rem(col + cols - 1, cols)), (row, lax.rem(col + 1, cols))
    has_above, has_below = row > 0, row < rows - 1
    has_before, has_after = col > 0, col < cols - 1

    barrier = pltpu.get_barrier_semaphore()
    for device in (above, below, before, after):
        pl.semaphore_signal(barrier, inc=1, device_id=device, device_id_type=MESH)
    pl.semaphore_wait(barrier, 4)

    count = [0]
    everything, waited = [], []

    def send(source, target, device):
        number = count[0]
        count[0] += 1
        copy = pltpu.make_async_remote_copy(
            src_ref=source, dst_ref=target, send_sem=send_sem.at[number], recv_sem=recv_sem.at[number],
            device_id=device, device_id_type=MESH,
        )
        copy.start()
        everything.append(copy)
        return copy

    def send_rows(source, target, low, high, low_to, high_to, depth, source_lane, target_lane, block):
        a = slice(source_lane + 128 * block, source_lane + 128 * block + 128)
        b = slice(target_lane + 128 * block, target_lane + 128 * block + 128)
        return [
            send(source.at[:, low : low + depth, a], target(0).at[:, low_to : low_to + depth, b], above),
            send(source.at[:, high : high + depth, a], target(1).at[:, high_to : high_to + depth, b], below),
        ]

    own_lanes = ((OWN, 0), (OWN + 256, 32))
    margin_lanes = ((0, 32), (OWN + TILE, 0))

    def send_cols(way, source, lanes, groups, depth, sends, recvs):
        pack(source, *lanes[way], groups, depth, sends.at[way])
        return [send(sends.at[way], recvs.at[way], after if way else before)]

    def arrived(*lists):
        for copies in lists:
            for copy in copies:
                copy.wait_recv()

    def place_halo(way, recvs, groups, depth):
        for part in range(2):
            for g, start in enumerate(groups):
                if way:
                    ext[part, start : start + depth, :OWN] = unpack(
                        recvs.at[1], 32, depth, part, g, has_before
                    )
                else:
                    ext[part, start : start + depth, OWN + TILE :] = unpack(
                        recvs.at[0], 0, depth, part, g, has_after
                    )

    def add_cols(way, recvs, groups, depth):
        for part in range(2):
            for g, start in enumerate(groups):
                if way:
                    canvas[part, start : start + depth, BLOCKS[0]] += unpack(
                        recvs.at[1], 0, depth, part, g, has_before
                    )
                else:
                    canvas[part, start : start + depth, BLOCKS[2]] += unpack(
                        recvs.at[0], 32, depth, part, g, has_after
                    )

    def send_obj(block):
        return send_rows(obj, lambda _: ext, 0, TILE - MARGIN, MARGIN + TILE, 0, MARGIN, 0, OWN, block)

    def gradients(j):
        for i in range(2):
            window(ext, canvas, probes, amps, tables, *shifts[2 * i + j], 2 * i + j)

    obj_rows = {0: send_obj(0), 2: send_obj(2)}
    ext[:, MARGIN : MARGIN + TILE, OWN : OWN + TILE] = obj[...]
    own_right = send_cols(1, ext, own_lanes, *OWN_ROWS, own_send, own_recv)
    obj_rows[1] = send_obj(1)

    shifts = []
    for number in range(4):
        i, j = number // 2, number % 2
        shifts.append((offsets[i, j, 0], offsets[i, j, 1] + 32 + 64 * j))
    for number in range(4):
        for part in range(2):
            probes[number, part] = rolled(
                rolled(probe[part], shifts[number][0], 0), shifts[number][1], 1
            )
        i, j = number // 2, number % 2
        pattern = amplitudes[i * WIN : (i + 1) * WIN, j * WIN : (j + 1) * WIN]
        pattern = sum(dot(piece, parity[0]) for piece in thirds(pattern))
        amps[number] = sum(dot(parity[1], piece) for piece in thirds(pattern))
    canvas[...] = jnp.zeros_like(canvas)

    def settle_rows(block):
        arrived(obj_rows[block])
        lanes = BLOCKS[block]
        for start, keep in ((0, has_above), (MARGIN + TILE, has_below)):
            halo = ext[:, start : start + MARGIN, lanes]
            ext[:, start : start + MARGIN, lanes] = jnp.where(keep, halo, 0.0)

    settle_rows(2)
    corner_right = send_cols(1, ext, own_lanes, *CORNER_ROWS, corner_send, corner_recv)
    own_left = send_cols(0, ext, own_lanes, *OWN_ROWS, own_send, own_recv)
    settle_rows(0)
    corner_left = send_cols(0, ext, own_lanes, *CORNER_ROWS, corner_send, corner_recv)
    settle_rows(1)
    arrived(own_right)
    place_halo(1, own_recv, *OWN_ROWS)
    arrived(corner_right)
    place_halo(1, corner_recv, *CORNER_ROWS)
    gradients(0)
    edge_left = send_cols(0, canvas, margin_lanes, *EDGE_ROWS, grad_edge_send, grad_edge_recv)
    mid_left = send_cols(0, canvas, margin_lanes, *MID_ROWS, grad_mid_send, grad_mid_recv)
    arrived(own_left)
    place_halo(0, own_recv, *OWN_ROWS)
    arrived(corner_left)
    place_halo(0, corner_recv, *CORNER_ROWS)
    gradients(1)
    edge_right = send_cols(1, canvas, margin_lanes, *EDGE_ROWS, grad_edge_send, grad_edge_recv)
    mid_right = send_cols(1, canvas, margin_lanes, *MID_ROWS, grad_mid_send, grad_mid_recv)

    def add_tv(number, carry):
        start = pl.multiple_of(number * 48, 8)
        for part, value in enumerate(tv_rows(ext, start, 48)):
            canvas[part, pl.ds(MARGIN + start, 48), OWN : OWN + TILE] += tv_weight * value
        return carry

    lax.fori_loop(0, 8, add_tv, 0)

    def send_shared(block, part):
        lanes = slice(128 * block, 128 * block + 128)
        return [
            send(canvas.at[part, :192, BLOCKS[block]], rows_recv.at[0, part, :, lanes], above),
            send(canvas.at[part, 384:, BLOCKS[block]], rows_recv.at[1, part, :, lanes], below),
        ]

    def taken_rows(block, part):
        theirs = slice(128 * block, 128 * block + 128)
        for start, source, keep, halo in ((384, 0, has_below, 480), (0, 1, has_above, 0)):
            inner = 384 if start else 96
            for first in (halo, inner):
                at = first - start
                total = canvas[part, first : first + 96, BLOCKS[block]] + jnp.where(
                    keep, rows_recv[source, part, at : at + 96, theirs], 0.0
                )
                if first == halo:
                    total = jnp.where(keep, total, 0.0)
                ext[part, first : first + 96, BLOCKS[block]] -= step_size * total

    shared = {(1, 0): send_shared(1, 0)}
    arrived(edge_left)
    add_cols(0, grad_edge_recv, *EDGE_ROWS)
    for part in range(2):
        shared[2, part] = send_shared(2, part)
    arrived(edge_right)
    add_cols(1, grad_edge_recv, *EDGE_ROWS)
    for part in range(2):
        shared[0, part] = send_shared(0, part)
    shared[1, 1] = send_shared(1, 1)
    arrived(mid_left)
    add_cols(0, grad_mid_recv, *MID_ROWS)
    arrived(mid_right)
    add_cols(1, grad_mid_recv, *MID_ROWS)
    ext[:, 192:384, OWN : OWN + TILE] -= step_size * canvas[:, 192:384, OWN : OWN + TILE]
    halo_mid_right = send_cols(1, ext, own_lanes, *MID_ROWS, halo_mid_send, halo_mid_recv)
    for part in range(2):
        arrived(shared[2, part])
        taken_rows(2, part)
    halo_edge_right = send_cols(1, ext, own_lanes, *EDGE_ROWS, halo_edge_send, halo_edge_recv)
    halo_mid_left = send_cols(0, ext, own_lanes, *MID_ROWS, halo_mid_send, halo_mid_recv)
    for part in range(2):
        arrived(shared[0, part])
        taken_rows(0, part)
    halo_edge_left = send_cols(0, ext, own_lanes, *EDGE_ROWS, halo_edge_send, halo_edge_recv)
    for part in range(2):
        arrived(shared[1, part])
        taken_rows(1, part)
    for copies in shared.values():
        for copy in copies:
            copy.wait_send()
            waited.append(copy)
    canvas[...] = jnp.zeros_like(canvas)
    arrived(halo_mid_right)
    place_halo(1, halo_mid_recv, *MID_ROWS)
    arrived(halo_edge_right)
    place_halo(1, halo_edge_recv, *EDGE_ROWS)
    gradients(0)
    edge_left = send_cols(0, canvas, margin_lanes, *EDGE_ROWS, last_edge_send, last_edge_recv)
    mid_left = send_cols(0, canvas, margin_lanes, *MID_ROWS, last_mid_send, last_mid_recv)
    arrived(halo_mid_left)
    place_halo(0, halo_mid_recv, *MID_ROWS)
    arrived(halo_edge_left)
    place_halo(0, halo_edge_recv, *EDGE_ROWS)
    gradients(1)
    edge_right = send_cols(1, canvas, margin_lanes, *EDGE_ROWS, last_edge_send, last_edge_recv)
    mid_right = send_cols(1, canvas, margin_lanes, *MID_ROWS, last_mid_send, last_mid_recv)

    def send_last(block):
        return send_rows(
            canvas, lambda k: last_rows_recv.at[k], 0, MARGIN + TILE, 0, 0, MARGIN, OWN, 0, block
        )

    last_rows = {1: send_last(1)}

    def start_out(number, carry):
        start = pl.multiple_of(number * 48, 8)
        here = pl.ds(MARGIN + start, 48)
        for part, value in enumerate(tv_rows(ext, start, 48)):
            out[part, pl.ds(start, 48), :] = (
                ext[part, here, OWN : OWN + TILE] - (step_size * tv_weight) * value
            )
        return carry

    lax.fori_loop(0, 8, start_out, 0)
    arrived(edge_left)
    add_cols(0, last_edge_recv, *EDGE_ROWS)
    last_rows[2] = send_last(2)
    arrived(edge_right)
    add_cols(1, last_edge_recv, *EDGE_ROWS)
    last_rows[0] = send_last(0)
    arrived(mid_left)
    add_cols(0, last_mid_recv, *MID_ROWS)
    arrived(mid_right)
    add_cols(1, last_mid_recv, *MID_ROWS)
    out[...] -= step_size * canvas[:, MARGIN : MARGIN + TILE, OWN : OWN + TILE]
    for block in (1, 2, 0):
        arrived(last_rows[block])
        lanes = slice(128 * block, 128 * block + 128)
        for start, source, keep in ((TILE - MARGIN, 0, has_below), (0, 1, has_above)):
            theirs = jnp.where(keep, last_rows_recv[source, :, :, lanes], 0.0)
            out[:, start : start + MARGIN, lanes] -= step_size * theirs
    for copy in everything:
        if not any(copy is other for other in waited):
            copy.wait_send()


def on_device(object_field, probe, amplitudes, offsets):
    vmem = pl.BlockSpec(memory_space=pltpu.VMEM)

    def pair(depth):
        return [pltpu.VMEM((2, 2, depth, 128), jnp.float32)] * 2

    return pl.pallas_call(
        kernel,
        out_shape=jax.ShapeDtypeStruct((2, TILE, TILE), jnp.float32),
        in_specs=[pl.BlockSpec(memory_space=pltpu.SMEM)] + [vmem] * 5,
        out_specs=vmem,
        scratch_shapes=[
            pltpu.VMEM((2, ROWS, COLS), jnp.float32),
            pltpu.VMEM((2, ROWS, COLS), jnp.float32),
            pltpu.VMEM((4, 2, WIN, WIN), jnp.float32),
            pltpu.VMEM((4, WIN, WIN), jnp.float32),
            *pair(288), *pair(144),
            *pair(288), *pair(144),
            pltpu.VMEM((2, 2, 192, TILE), jnp.float32),
            *pair(144), *pair(288),
            *pair(288), *pair(144),
            pltpu.VMEM((2, 2, MARGIN, TILE), jnp.float32),
            pltpu.SemaphoreType.DMA((40,)),
            pltpu.SemaphoreType.DMA((40,)),
        ],
        compiler_params=pltpu.CompilerParams(
            collective_id=0, has_side_effects=True, vmem_limit_bytes=56 << 20
        ),
        name="ptycho",
    )(offsets, object_field, probe, amplitudes, jnp.asarray(dft_tables()), jnp.asarray(parity_table()))


def solution(mesh):
    in_specs = (P(None, "row", "col"), P(), P("row", "col"), P("row", "col", None))
    out_specs = P(None, "row", "col")
    return jax.shard_map(
        on_device, mesh=mesh, in_specs=in_specs, out_specs=out_specs, check_vma=False
    )
```

```python
import functools

import jax
import jax.numpy as jnp
import ml_dtypes
import numpy as np
from jax import lax
from jax.experimental import pallas as pl
from jax.experimental.pallas import tpu as pltpu
from jax.sharding import PartitionSpec as P

WIN = 256
HALF = 128
MARGIN = 96
PITCH = 192
TILE = 384
ROWS = PITCH + 2 * MARGIN
COLS = 1024
OWN = 128
WIDE = 2 * TILE
BASES = (0, 128, 384, 512)

step_size = 0.3
tv_weight = 0.2
tv_smooth = 0.1
amp_floor = 0.5

MESH = pl.DeviceIdType.MESH


def dft_tables():
    n = np.arange(HALF)
    whole = []
    for odd in (0, 1):
        k = 2 * np.arange(HALF) + odd
        angle = 2.0 * np.pi * ((k[:, None] * n[None, :]) % WIN) / WIN
        cosine = np.cos(angle) / 16.0
        sine = np.sin(angle) / 16.0
        left_form = np.block([[cosine, sine], [-sine, cosine]])
        whole += [left_form, left_form.T]
    high = [m.astype(ml_dtypes.bfloat16) for m in whole]
    low = [(m - h.astype(np.float64)).astype(ml_dtypes.bfloat16) for m, h in zip(whole, high)]
    return np.stack(high + low)


def parity_table():
    table = np.zeros((WIN, WIN), ml_dtypes.bfloat16)
    order = np.concatenate([np.arange(0, WIN, 2), np.arange(1, WIN, 2)])
    table[order, np.arange(WIN)] = 1.0
    return np.stack([table, table.T])


def split(x):
    high = x.astype(jnp.bfloat16)
    return high, (x - high.astype(jnp.float32)).astype(jnp.bfloat16)


def thirds(x):
    high = x.astype(jnp.bfloat16)
    return high, *split(x - high.astype(jnp.float32))


def dot(a, b):
    return jnp.dot(a, b, preferred_element_type=jnp.float32)


def cat(a, b, axis):
    return jnp.concatenate([a, b], axis=axis)


def left(tables, k, x):
    high, low = split(x)
    return dot(tables[k], high) + dot(tables[k], low) + dot(tables[k + 4], high)


def right(x, tables, k):
    high, low = split(x)
    return dot(high, tables[k]) + dot(low, tables[k]) + dot(high, tables[k + 4])


def fitted(spectrum, amp):
    re, im = spectrum[:, :HALF], spectrum[:, HALF:]
    magnitude = jnp.sqrt(re * re + im * im)
    keeping = 1.0 - amp / jnp.maximum(magnitude, amp_floor)
    return cat(re * keeping, im * keeping, 1)


def back_field(re, im, amp, tables):
    even = left(tables, 0, cat(re[:HALF] + re[HALF:], im[:HALF] + im[HALF:], 0))
    odd = left(tables, 2, cat(re[:HALF] - re[HALF:], im[:HALF] - im[HALF:], 0))
    re, im = cat(even[:HALF], odd[:HALF], 0), cat(even[HALF:], odd[HALF:], 0)
    even = cat(re[:, :HALF] + re[:, HALF:], im[:, :HALF] + im[:, HALF:], 1)
    odd = cat(re[:, :HALF] - re[:, HALF:], im[:, :HALF] - im[:, HALF:], 1)
    even = fitted(right(even, tables, 1), amp[:, :HALF])
    odd = fitted(right(odd, tables, 3), amp[:, HALF:])
    u, v = right(even, tables, 0), right(odd, tables, 2)
    p, m = u + v, u - v
    re, im = cat(p[:, :HALF], m[:, :HALF], 1), cat(p[:, HALF:], m[:, HALF:], 1)
    u = left(tables, 1, cat(re[:HALF], im[:HALF], 0))
    v = left(tables, 3, cat(re[HALF:], im[HALF:], 0))
    p, m = u + v, u - v
    return cat(p[:HALF], m[:HALF], 0), cat(p[HALF:], m[HALF:], 0)


def spread(plane, shape):
    return jnp.broadcast_to(cat(plane[0:1, :], plane[0:1, :], 1), shape)


def window(ext, canvas, probes, amps, tables, shifts, number):
    first = BASES[number]
    shape = (HALF, WIN)
    by_row = lax.broadcasted_iota(jnp.int32, shape, 0) >= spread(shifts[number, 0], shape)
    by_col = lax.broadcasted_iota(jnp.int32, shape, 1) >= spread(shifts[number, 1], shape)

    def rows_at(part, start):
        near = ext[part, start : start + HALF, first : first + WIN]
        far = ext[part, start : start + HALF, first + WIN : first + 2 * WIN]
        return jnp.where(by_col, near, far)

    def cells(part):
        upper = jnp.where(by_row, rows_at(part, 0), rows_at(part, WIN))
        return cat(upper, rows_at(part, HALF), 0)

    re, im = cells(0), cells(1)
    probe_re, probe_im = probes[number, 0], probes[number, 1]
    back_re, back_im = back_field(
        probe_re * re - probe_im * im, probe_re * im + probe_im * re, amps[number], tables
    )
    grads = (probe_re * back_re + probe_im * back_im, probe_re * back_im - probe_im * back_re)
    for part, grad in enumerate(grads):
        upper, lower = grad[:HALF], grad[HALF:]
        for start, value in (
            (0, jnp.where(by_row, upper, 0.0)),
            (HALF, lower),
            (WIN, jnp.where(by_row, 0.0, upper)),
        ):
            canvas[part, start : start + HALF, first : first + WIN] += jnp.where(by_col, value, 0.0)
            canvas[part, start : start + HALF, first + WIN : first + 2 * WIN] += jnp.where(
                by_col, 0.0, value
            )


def rolled(x, amount, axis):
    for bit in range(8):
        x = jnp.where((amount & (1 << bit)) != 0, pltpu.roll(x, 1 << bit, axis), x)
    return x


def lane_part(depth):
    return lax.broadcasted_iota(jnp.int32, (depth, 128), 1) // 32


def turned(x, amount):
    amount %= 128
    return pltpu.roll(x, amount, 1) if amount else x


def pack(source, lane, skip, start, depth, target):
    part_of = lane_part(depth)
    for part in range(2):
        groups = [
            source[part, pl.ds(pl.multiple_of(start + g * depth, 8), depth), lane : lane + 128]
            for g in range(4)
        ]
        for third in range(3):
            value = turned(groups[0], -32 * third - skip)
            for g in range(1, 4):
                value = jnp.where(part_of == g, turned(groups[g], 32 * (g - third) - skip), value)
            target[part, third * depth : (third + 1) * depth, :] = value


def unpack(source, skip, depth, part, g, keep):
    part_of = lane_part(depth)
    value = jnp.zeros((depth, 128), jnp.float32)
    for third in range(3):
        block = turned(source[part, third * depth : (third + 1) * depth, :], skip + 32 * (third - g))
        value = jnp.where(part_of == third + skip // 32, block, value)
    return jnp.where(keep, value, 0.0)


def tv_rows(ext, start, depth):
    high = depth + 16
    first = pl.multiple_of(MARGIN + start - 8, 8)
    fields = [ext[part, pl.ds(first, high), :] for part in range(2)]
    down = [pltpu.roll(f, high - 1, 0) - f for f in fields]
    right_ = [pltpu.roll(f, COLS - 1, 1) - f for f in fields]
    total = down[0] * down[0] + right_[0] * right_[0] + (down[1] * down[1] + right_[1] * right_[1])
    inverse = lax.rsqrt(total + tv_smooth)
    out = []
    for part in range(2):
        flow_down = down[part] * inverse
        flow_right = right_[part] * inverse
        value = pltpu.roll(flow_down, 1, 0) - flow_down + pltpu.roll(flow_right, 1, 1) - flow_right
        out.append(value[8 : depth + 8, OWN : OWN + WIDE])
    return out


def lanes_of(block):
    return slice(OWN + 128 * block, OWN + 128 * block + 128)


def kernel(
    offsets, obj, probe_in, amplitudes, tables_in, parity_in, out,
    ext, canvas, canvas_2, probes, amps, probe, tables, parity,
    planes, shifts, raw_amps,
    first_send, first_recv, halo_send, halo_recv,
    grad_send, grad_recv, next_send, next_recv, last_send, last_recv,
    rows_recv, pair_recv, result, result_recv,
    send_sem, recv_sem, load_sem,
):
    row, col = lax.axis_index("row"), lax.axis_index("col")
    rows, cols = lax.axis_size("row"), lax.axis_size("col")
    quad, low, core = col // 4, lax.rem(col // 2, 2), lax.rem(col, 2)
    quads = cols // 4

    def device(at_row, at_quad, at_low, at_core):
        return (
            lax.rem(at_row + rows, rows),
            4 * lax.rem(at_quad + quads, quads) + 2 * at_low + at_core,
        )

    holder = [device(row, quad, core, k) for k in range(2)]
    holder_here = [(low == core) & (core == k) for k in range(2)]
    taker = [device(row, quad, k, low) for k in range(2)]
    taker_here = [(low == k) & (core == k) for k in range(2)]
    above = device(row - 1 + low, quad, 1 - low, core)
    below = device(row + low, quad, 1 - low, core)
    pair = device(row - 1 + 2 * low, quad, 1 - low, core)
    before = device(row, quad - 1 + core, low, 1 - core)
    after = device(row, quad + core, low, 1 - core)
    across = device(row, quad - 1 + 2 * core, low, 1 - core)
    has_above = (row > 0) | (low > 0)
    has_below = (row < rows - 1) | (low == 0)
    has_pair = ((low == 0) & (row > 0)) | ((low == 1) & (row < rows - 1))
    has_before = (quad > 0) | (core > 0)
    has_after = (quad < quads - 1) | (core == 0)

    loads = [
        pltpu.make_async_copy(source, target, load_sem.at[k])
        for k, (source, target) in enumerate(
            ((probe_in, probe), (parity_in, parity), (tables_in, tables))
        )
    ]
    for load in loads:
        load.start()
    barrier = pltpu.get_barrier_semaphore()
    for other in (
        device(row, quad, low, 1 - core), device(row, quad, 1 - low, core),
        device(row, quad, 1 - low, 1 - core), pair, across,
    ):
        pl.semaphore_signal(barrier, inc=1, device_id=other, device_id_type=MESH)
    pl.semaphore_wait(barrier, 5)

    sent, taken = [0], [0]
    ends = []

    def slots(count):
        taken[0] += count
        return taken[0] - count

    def send(source, target, other, slot, here=None):
        number = sent[0]
        sent[0] += 1
        remote = pltpu.make_async_remote_copy(
            src_ref=source, dst_ref=target, send_sem=send_sem.at[number], recv_sem=recv_sem.at[slot],
            device_id=other, device_id_type=MESH,
        )
        if here is None:
            remote.start()
            ends.append(remote.wait_send)
            return remote.wait_send
        local = pltpu.make_async_copy(source, target, recv_sem.at[slot])
        pl.when(here)(local.start)
        pl.when(jnp.logical_not(here))(remote.start)
        ends.append(lambda: pl.when(jnp.logical_not(here))(remote.wait_send))

    def arrived(target, slot):
        pltpu.make_async_copy(target, target, recv_sem.at[slot]).wait()

    def rows_from(start, depth):
        return pl.ds(pl.multiple_of(start, 8), depth)

    my_tile = pl.ds(pl.multiple_of(OWN + TILE * core, 128), TILE)

    def tile_lanes(k):
        return slice(OWN + TILE * k, OWN + TILE * k + TILE)

    for i in range(2):
        for j in range(2):
            planes[i, j, 0] = jnp.full((8, 128), offsets[i, j, 0], jnp.int32)
            planes[i, j, 1] = jnp.full((8, 128), offsets[i, j, 1] + (32 + 64 * j), jnp.int32)
    shift_slot, near_slot, far_slot = slots(2), slots(2), slots(2)
    two = pl.ds(2 * core, 2)
    for k in range(2):
        send(planes.at[k], shifts.at[two], taker[k], shift_slot + core, taker_here[k])
    for k, (start, to) in enumerate(((0, 96), (288, 192))):
        send(
            obj.at[:, start : start + 96, :], ext.at[:, to : to + 96, my_tile],
            taker[k], near_slot + core, taker_here[k],
        )
    for k, to in enumerate((192, 0)):
        send(
            obj.at[:, 96:288, :], ext.at[:, to : to + 192, my_tile],
            taker[k], far_slot + core, taker_here[k],
        )

    canvas[...] = jnp.zeros_like(canvas)
    canvas_2[...] = jnp.zeros_like(canvas_2)
    for k in range(2):
        arrived(shifts.at[2 * k : 2 * k + 2], shift_slot + k)

    edge = MARGIN + MARGIN * low
    halo = 288 * low
    pair_slot = slots(2)
    from_ext = []
    for k in range(2):
        arrived(ext.at[:, 0:96, tile_lanes(k)], near_slot + k)
        from_ext.append(
            send(
                ext.at[:, rows_from(edge, 96), tile_lanes(k)],
                ext.at[:, rows_from(288 - halo, 96), tile_lanes(k)], pair, pair_slot + k,
            )
        )
    amp_slot = slots(4)
    for j in range(2):
        for k in range(2):
            send(
                amplitudes.at[k * WIN : (k + 1) * WIN, j * WIN : (j + 1) * WIN],
                raw_amps.at[2 * core + j], taker[k], amp_slot + 2 * core + j, taker_here[k],
            )

    loads[0].wait()
    for number in range(4):
        for part in range(2):
            turn = [spread(shifts[number, axis], (WIN, WIN)) for axis in range(2)]
            probes[number, part] = rolled(rolled(probe[part], turn[0], 0), turn[1], 1)
    for load in loads[1:]:
        load.wait()

    own_lanes = ((OWN, 0), (OWN + WIDE - 128, 32))
    margin_lanes = ((0, 32), (OWN + WIDE, 0))

    def send_cols(way, source, lanes, start, depth, sends, recvs, slot):
        pack(source, *lanes[way], start, depth, sends.at[way])
        send(sends.at[way], recvs.at[way], after if way else before, slot + way)

    def place_halo(way, recvs, start, depth, slot):
        arrived(recvs.at[way], slot + way)
        for part in range(2):
            for g in range(4):
                here = rows_from(start + g * depth, depth)
                if way:
                    ext[part, here, :OWN] = unpack(recvs.at[1], 32, depth, part, g, has_before)
                else:
                    ext[part, here, OWN + WIDE :] = unpack(recvs.at[0], 0, depth, part, g, has_after)

    def add_cols(way, target, recvs, slot):
        arrived(recvs.at[way], slot + way)
        for part in range(2):
            for g in range(4):
                here = slice(96 * g, 96 * g + 96)
                if way:
                    target[part, here, lanes_of(0)] += unpack(recvs.at[1], 0, 96, part, g, has_before)
                else:
                    target[part, here, lanes_of(5)] += unpack(recvs.at[0], 32, 96, part, g, has_after)

    first_slot, halo_slot = slots(2), slots(2)
    most = MARGIN - MARGIN * low
    for k in range(2):
        arrived(ext.at[:, 0:192, tile_lanes(k)], far_slot + k)
    for way in (1, 0):
        send_cols(way, ext, own_lanes, most, 72, first_send, first_recv, first_slot)
    for k in range(2):
        arrived(ext.at[:, 0:96, tile_lanes(k)], pair_slot + k)
    here = rows_from(halo, 96)
    ext[:, here, OWN : OWN + WIDE] = jnp.where(has_pair, ext[:, here, OWN : OWN + WIDE], 0.0)
    for way in (1, 0):
        send_cols(way, ext, own_lanes, halo, 24, halo_send, halo_recv, halo_slot)

    def permuted(number):
        arrived(raw_amps.at[number], amp_slot + number)
        pattern = sum(dot(piece, parity[0]) for piece in thirds(raw_amps[number]))
        amps[number] = sum(dot(parity[1], piece) for piece in thirds(pattern))

    def gradient(target, number):
        window(ext, target, probes, amps, tables, shifts, number)

    def add_tv(number, carry):
        start = number * 48
        here = rows_from(MARGIN + start, 48)
        for part, value in enumerate(tv_rows(ext, start, 48)):
            canvas[part, here, OWN : OWN + WIDE] += tv_weight * value
        return carry

    row_slot = slots(12)

    def send_block(block):
        lanes = slice(128 * block, 128 * block + 128)
        slot = row_slot + 2 * block
        send(canvas.at[:, :192, lanes_of(block)], rows_recv.at[0, :, :, lanes], above, slot)
        send(canvas.at[:, 192:, lanes_of(block)], rows_recv.at[1, :, :, lanes], below, slot + 1)

    def take_block(block):
        theirs = slice(128 * block, 128 * block + 128)
        for source, keep, starts in ((1, has_above, (0, 96)), (0, has_below, (288, 192))):
            arrived(rows_recv.at[source, :, :, theirs], row_slot + 2 * block + source)
            for start in starts:
                at = start % 192
                for part in range(2):
                    total = canvas[part, start : start + 96, lanes_of(block)] + jnp.where(
                        keep, rows_recv[source, part, at : at + 96, theirs], 0.0
                    )
                    if start in (0, 288):
                        total = jnp.where(keep, total, 0.0)
                    ext[part, start : start + 96, lanes_of(block)] -= step_size * total

    place_halo(1, first_recv, most, 72, first_slot)
    place_halo(1, halo_recv, halo, 24, halo_slot)
    permuted(0)
    gradient(canvas, 0)
    grad_slot = slots(2)
    send_cols(0, canvas, margin_lanes, 0, 96, grad_send, grad_recv, grad_slot)
    permuted(1)
    gradient(canvas, 1)
    place_halo(0, first_recv, most, 72, first_slot)
    place_halo(0, halo_recv, halo, 24, halo_slot)
    lax.fori_loop(0, 4, add_tv, 0)
    send_block(1)
    permuted(2)
    gradient(canvas, 2)
    permuted(3)
    gradient(canvas, 3)
    send_cols(1, canvas, margin_lanes, 0, 96, grad_send, grad_recv, grad_slot)
    add_cols(0, canvas, grad_recv, grad_slot)
    send_block(5)
    send_block(2)
    add_cols(1, canvas, grad_recv, grad_slot)
    send_block(0)
    send_block(3)
    send_block(4)
    next_slot = slots(2)
    for end in from_ext:
        end()
        ends.remove(end)
    take_block(1)
    take_block(5)
    send_cols(1, ext, own_lanes, 0, 96, next_send, next_recv, next_slot)
    take_block(2)
    take_block(0)
    send_cols(0, ext, own_lanes, 0, 96, next_send, next_recv, next_slot)
    place_halo(1, next_recv, 0, 96, next_slot)
    gradient(canvas_2, 0)
    last_slot = slots(2)
    send_cols(0, canvas_2, margin_lanes, 0, 96, last_send, last_recv, last_slot)
    take_block(3)
    gradient(canvas_2, 1)
    take_block(4)
    gradient(canvas_2, 2)
    place_halo(0, next_recv, 0, 96, next_slot)
    gradient(canvas_2, 3)
    send_cols(1, canvas_2, margin_lanes, 0, 96, last_send, last_recv, last_slot)

    sum_slot, main_slot, rest_slot = slots(2), slots(4), slots(4)

    def send_pair(k):
        send(
            canvas_2.at[:, rows_from(halo, 96), tile_lanes(k)],
            pair_recv.at[:, :, TILE * k : TILE * k + TILE], pair, sum_slot + k,
        )

    def send_main(k):
        send(
            result.at[:, rows_from(192 - 192 * low, 192), TILE * k : TILE * k + TILE],
            result_recv.at[low], holder[k], main_slot + low, holder_here[k],
        )

    def finish(k):
        lanes = slice(TILE * k, TILE * k + TILE)
        result[:, :, lanes] -= step_size * canvas_2[:, :, tile_lanes(k)]

    def start_result(number, carry):
        start = number * 48
        here = rows_from(MARGIN + start, 48)
        for part, value in enumerate(tv_rows(ext, start, 48)):
            result[part, here, :] = ext[part, here, OWN : OWN + WIDE] - (step_size * tv_weight) * value
        return carry

    add_cols(0, canvas_2, last_recv, last_slot)
    send_pair(1)
    result[:, :MARGIN, :] = jnp.zeros((2, MARGIN, WIDE), jnp.float32)
    result[:, MARGIN + PITCH :, :] = jnp.zeros((2, MARGIN, WIDE), jnp.float32)
    lax.fori_loop(0, 4, start_result, 0)
    finish(1)
    send_main(1)
    add_cols(1, canvas_2, last_recv, last_slot)
    send_pair(0)
    finish(0)
    send_main(0)
    for k in (1, 0):
        lanes = slice(TILE * k, TILE * k + TILE)
        arrived(pair_recv.at[:, :, lanes], sum_slot + k)
        here = rows_from(edge, 96)
        result[:, here, lanes] -= jnp.where(has_pair, step_size * pair_recv[:, :, lanes], 0.0)
        send(
            result.at[:, here, lanes], out.at[:, rows_from(halo, 96), :],
            holder[k], rest_slot + low, holder_here[k],
        )
    for k in range(2):
        arrived(result_recv.at[k], main_slot + k)
    out[:, 96:288, :] = result_recv[0] + result_recv[1]
    for k, start in enumerate((0, 288)):
        arrived(out.at[:, start : start + 96, :], rest_slot + k)
    for end in ends:
        end()


def on_device(object_field, probe, amplitudes, offsets):
    vmem = pl.BlockSpec(memory_space=pltpu.VMEM)
    left_there = pl.BlockSpec(memory_space=pl.ANY)

    def pair(depth):
        return [pltpu.VMEM((2, 2, depth, 128), jnp.float32)] * 2

    tables, parity = dft_tables(), parity_table()
    return pl.pallas_call(
        kernel,
        out_shape=jax.ShapeDtypeStruct((2, TILE, TILE), jnp.float32),
        in_specs=[pl.BlockSpec(memory_space=pltpu.SMEM)] + [left_there] * 5,
        out_specs=vmem,
        scratch_shapes=[
            pltpu.VMEM((2, ROWS, COLS), jnp.float32),
            pltpu.VMEM((2, ROWS, COLS), jnp.float32),
            pltpu.VMEM((2, ROWS, COLS), jnp.float32),
            pltpu.VMEM((4, 2, WIN, WIN), jnp.float32),
            pltpu.VMEM((4, WIN, WIN), jnp.float32),
            pltpu.VMEM(probe.shape, jnp.float32),
            pltpu.VMEM(tables.shape, jnp.bfloat16),
            pltpu.VMEM(parity.shape, jnp.bfloat16),
            pltpu.VMEM((2, 2, 2, 8, 128), jnp.int32),
            pltpu.VMEM((4, 2, 8, 128), jnp.int32),
            pltpu.VMEM((4, WIN, WIN), jnp.float32),
            *pair(216), *pair(72),
            *pair(288), *pair(288), *pair(288),
            pltpu.VMEM((2, 2, 192, WIDE), jnp.float32),
            pltpu.VMEM((2, MARGIN, WIDE), jnp.float32),
            pltpu.VMEM((2, ROWS, WIDE), jnp.float32),
            pltpu.VMEM((2, 2, 192, TILE), jnp.float32),
            pltpu.SemaphoreType.DMA((64,)),
            pltpu.SemaphoreType.DMA((64,)),
            pltpu.SemaphoreType.DMA((3,)),
        ],
        compiler_params=pltpu.CompilerParams(
            collective_id=0, has_side_effects=True, vmem_limit_bytes=58 << 20
        ),
        name="ptycho",
    )(offsets, object_field, probe, amplitudes, jnp.asarray(tables), jnp.asarray(parity))


def solution(mesh):
    in_specs = (P(None, "row", "col"), P(), P("row", "col"), P("row", "col", None))
    out_specs = P(None, "row", "col")
    return jax.shard_map(
        on_device, mesh=mesh, in_specs=in_specs, out_specs=out_specs, check_vma=False
    )
```

```python
import functools

import jax
import jax.numpy as jnp
import ml_dtypes
import numpy as np
from jax import lax
from jax.experimental import pallas as pl
from jax.experimental.pallas import tpu as pltpu
from jax.sharding import PartitionSpec as P

WIN = 256
HALF = 128
MARGIN = 96
PITCH = 192
TILE = 384
ROWS = PITCH + 2 * MARGIN
COLS = 1024
OWN = 128
WIDE = 2 * TILE
HALF_LANES = TILE + 256
BASES = (0, 128, 384, 512)

step_size = 0.3
tv_weight = 0.2
tv_smooth = 0.1
amp_floor = 0.5

MESH = pl.DeviceIdType.MESH


def dft_tables():
    n = np.arange(HALF)
    whole = []
    for odd in (0, 1):
        k = 2 * np.arange(HALF) + odd
        angle = 2.0 * np.pi * ((k[:, None] * n[None, :]) % WIN) / WIN
        cosine = np.cos(angle) / 16.0
        sine = np.sin(angle) / 16.0
        left_form = np.block([[cosine, sine], [-sine, cosine]])
        whole += [left_form, left_form.T]
    high = [m.astype(ml_dtypes.bfloat16) for m in whole]
    low = [(m - h.astype(np.float64)).astype(ml_dtypes.bfloat16) for m, h in zip(whole, high)]
    return np.stack(high + low)


def parity_table():
    table = np.zeros((WIN, WIN), ml_dtypes.bfloat16)
    order = np.concatenate([np.arange(0, WIN, 2), np.arange(1, WIN, 2)])
    table[order, np.arange(WIN)] = 1.0
    return np.stack([table, table.T])


def split(x):
    high = x.astype(jnp.bfloat16)
    return high, (x - high.astype(jnp.float32)).astype(jnp.bfloat16)


def dot(a, b):
    return jnp.dot(a, b, preferred_element_type=jnp.float32)


def cat(a, b, axis):
    return jnp.concatenate([a, b], axis=axis)


def left(tables, k, x):
    high, low = split(x)
    return dot(tables[k], high) + dot(tables[k], low) + dot(tables[k + 4], high)


def right(x, tables, k):
    high, low = split(x)
    return dot(high, tables[k]) + dot(low, tables[k]) + dot(high, tables[k + 4])


def fitted(spectrum, amp):
    re, im = spectrum[:, :HALF], spectrum[:, HALF:]
    magnitude = jnp.sqrt(re * re + im * im)
    keeping = 1.0 - amp / jnp.maximum(magnitude, amp_floor)
    return cat(re * keeping, im * keeping, 1)


def back_field(re, im, amp, tables):
    even = left(tables, 0, cat(re[:HALF] + re[HALF:], im[:HALF] + im[HALF:], 0))
    odd = left(tables, 2, cat(re[:HALF] - re[HALF:], im[:HALF] - im[HALF:], 0))
    re, im = cat(even[:HALF], odd[:HALF], 0), cat(even[HALF:], odd[HALF:], 0)
    even = cat(re[:, :HALF] + re[:, HALF:], im[:, :HALF] + im[:, HALF:], 1)
    odd = cat(re[:, :HALF] - re[:, HALF:], im[:, :HALF] - im[:, HALF:], 1)
    even = fitted(right(even, tables, 1), amp[:, :HALF])
    odd = fitted(right(odd, tables, 3), amp[:, HALF:])
    u, v = right(even, tables, 0), right(odd, tables, 2)
    p, m = u + v, u - v
    re, im = cat(p[:, :HALF], m[:, :HALF], 1), cat(p[:, HALF:], m[:, HALF:], 1)
    u = left(tables, 1, cat(re[:HALF], im[:HALF], 0))
    v = left(tables, 3, cat(re[HALF:], im[HALF:], 0))
    p, m = u + v, u - v
    return cat(p[:HALF], m[:HALF], 0), cat(p[HALF:], m[HALF:], 0)


def spread(plane, shape):
    return jnp.broadcast_to(cat(plane[0:1, :], plane[0:1, :], 1), shape)


def window(ext, canvas, probes, amps, tables, shifts, number):
    first = BASES[number]
    shape = (HALF, WIN)
    by_row = lax.broadcasted_iota(jnp.int32, shape, 0) >= spread(shifts[number, 0], shape)
    by_col = lax.broadcasted_iota(jnp.int32, shape, 1) >= spread(shifts[number, 1], shape)

    def rows_at(part, start):
        near = ext[part, start : start + HALF, first : first + WIN]
        far = ext[part, start : start + HALF, first + WIN : first + 2 * WIN]
        return jnp.where(by_col, near, far)

    def cells(part):
        upper = jnp.where(by_row, rows_at(part, 0), rows_at(part, WIN))
        return cat(upper, rows_at(part, HALF), 0)

    re, im = cells(0), cells(1)
    probe_re, probe_im = probes[number, 0], probes[number, 1]
    back_re, back_im = back_field(
        probe_re * re - probe_im * im, probe_re * im + probe_im * re, amps[number], tables
    )
    grads = (probe_re * back_re + probe_im * back_im, probe_re * back_im - probe_im * back_re)
    for part, grad in enumerate(grads):
        upper, lower = grad[:HALF], grad[HALF:]
        for start, value in (
            (0, jnp.where(by_row, upper, 0.0)),
            (HALF, lower),
            (WIN, jnp.where(by_row, 0.0, upper)),
        ):
            canvas[part, start : start + HALF, first : first + WIN] += jnp.where(by_col, value, 0.0)
            canvas[part, start : start + HALF, first + WIN : first + 2 * WIN] += jnp.where(
                by_col, 0.0, value
            )


def rolled(x, amount, axis):
    for bit in range(8):
        x = jnp.where((amount & (1 << bit)) != 0, pltpu.roll(x, 1 << bit, axis), x)
    return x


def lane_part(depth):
    return lax.broadcasted_iota(jnp.int32, (depth, 128), 1) // 32


def turned(x, amount):
    amount %= 128
    return pltpu.roll(x, amount, 1) if amount else x


def pack(source, lane, skip, start, depth, target):
    part_of = lane_part(depth)
    for part in range(2):
        groups = [
            source[part, pl.ds(pl.multiple_of(start + g * depth, 8), depth), lane : lane + 128]
            for g in range(4)
        ]
        for third in range(3):
            value = turned(groups[0], -32 * third - skip)
            for g in range(1, 4):
                value = jnp.where(part_of == g, turned(groups[g], 32 * (g - third) - skip), value)
            target[part, third * depth : (third + 1) * depth, :] = value


def unpack(source, skip, depth, part, g, keep):
    part_of = lane_part(depth)
    value = jnp.zeros((depth, 128), jnp.float32)
    for third in range(3):
        block = turned(source[part, third * depth : (third + 1) * depth, :], skip + 32 * (third - g))
        value = jnp.where(part_of == third + skip // 32, block, value)
    return jnp.where(keep, value, 0.0)


def tv_rows(ext, start, depth, side):
    high = depth + 16
    first = pl.multiple_of(MARGIN + start - 8, 8)
    lanes = slice(TILE * side, TILE * side + HALF_LANES)
    fields = [ext[part, pl.ds(first, high), lanes] for part in range(2)]
    down = [pltpu.roll(f, high - 1, 0) - f for f in fields]
    right_ = [pltpu.roll(f, HALF_LANES - 1, 1) - f for f in fields]
    total = down[0] * down[0] + right_[0] * right_[0] + (down[1] * down[1] + right_[1] * right_[1])
    inverse = lax.rsqrt(total + tv_smooth)
    out = []
    for part in range(2):
        flow_down = down[part] * inverse
        flow_right = right_[part] * inverse
        value = pltpu.roll(flow_down, 1, 0) - flow_down + pltpu.roll(flow_right, 1, 1) - flow_right
        out.append(value[8 : depth + 8, OWN : OWN + TILE])
    return out


def lanes_of(block):
    return slice(OWN + 128 * block, OWN + 128 * block + 128)


def kernel(
    offsets, obj, probe_in, amplitudes, tables_in, parity_in, out,
    ext, canvas, canvas_2, probes, amps, probe, tables, parity,
    planes, shifts, raw_amps,
    first_send, first_recv, halo_send, halo_recv,
    grad_send, grad_recv, next_send, next_recv, last_send, last_recv,
    rows_recv, pair_recv, result, result_recv,
    send_sem, recv_sem, load_sem,
):
    row, col = lax.axis_index("row"), lax.axis_index("col")
    rows, cols = lax.axis_size("row"), lax.axis_size("col")
    quad, low, core = col // 4, lax.rem(col // 2, 2), lax.rem(col, 2)
    quads = cols // 4

    def device(at_row, at_quad, at_low, at_core):
        return (
            lax.rem(at_row + rows, rows),
            4 * lax.rem(at_quad + quads, quads) + 2 * at_low + at_core,
        )

    holder = [device(row, quad, core, k) for k in range(2)]
    holder_here = [(low == core) & (core == k) for k in range(2)]
    taker = [device(row, quad, k, low) for k in range(2)]
    taker_here = [(low == k) & (core == k) for k in range(2)]
    above = device(row - 1 + low, quad, 1 - low, core)
    below = device(row + low, quad, 1 - low, core)
    pair = device(row - 1 + 2 * low, quad, 1 - low, core)
    before = device(row, quad - 1 + core, low, 1 - core)
    after = device(row, quad + core, low, 1 - core)
    across = device(row, quad - 1 + 2 * core, low, 1 - core)
    has_above = (row > 0) | (low > 0)
    has_below = (row < rows - 1) | (low == 0)
    has_pair = ((low == 0) & (row > 0)) | ((low == 1) & (row < rows - 1))
    has_before = (quad > 0) | (core > 0)
    has_after = (quad < quads - 1) | (core == 0)

    loads = [
        pltpu.make_async_copy(source, target, load_sem.at[k])
        for k, (source, target) in enumerate(
            ((probe_in, probe), (parity_in, parity), (tables_in, tables))
        )
    ]
    for load in loads:
        load.start()
    barrier = pltpu.get_barrier_semaphore()
    for other in (
        device(row, quad, low, 1 - core), device(row, quad, 1 - low, core),
        device(row, quad, 1 - low, 1 - core), pair, across,
    ):
        pl.semaphore_signal(barrier, inc=1, device_id=other, device_id_type=MESH)
    pl.semaphore_wait(barrier, 5)

    sent, taken = [0], [0]
    ends = []

    def slots(count):
        taken[0] += count
        return taken[0] - count

    def send(source, target, other, slot, here=None):
        number = sent[0]
        sent[0] += 1
        remote = pltpu.make_async_remote_copy(
            src_ref=source, dst_ref=target, send_sem=send_sem.at[number], recv_sem=recv_sem.at[slot],
            device_id=other, device_id_type=MESH,
        )
        if here is None:
            remote.start()
            ends.append(remote.wait_send)
            return remote.wait_send
        local = pltpu.make_async_copy(source, target, recv_sem.at[slot])
        pl.when(here)(local.start)
        pl.when(jnp.logical_not(here))(remote.start)
        ends.append(lambda: pl.when(jnp.logical_not(here))(remote.wait_send))

    def arrived(target, slot):
        pltpu.make_async_copy(target, target, recv_sem.at[slot]).wait()

    def rows_from(start, depth):
        return pl.ds(pl.multiple_of(start, 8), depth)

    my_tile = pl.ds(pl.multiple_of(OWN + TILE * core, 128), TILE)

    def tile_lanes(k):
        return slice(OWN + TILE * k, OWN + TILE * k + TILE)

    for i in range(2):
        for j in range(2):
            planes[i, j, 0] = jnp.full((8, 128), offsets[i, j, 0], jnp.int32)
            planes[i, j, 1] = jnp.full((8, 128), offsets[i, j, 1] + (32 + 64 * j), jnp.int32)
    shift_slot, near_slot, far_slot = slots(2), slots(2), slots(2)
    two = pl.ds(2 * core, 2)
    for k in range(2):
        send(planes.at[k], shifts.at[two], taker[k], shift_slot + core, taker_here[k])
    for k, (start, to) in enumerate(((0, 96), (288, 192))):
        send(
            obj.at[:, start : start + 96, :], ext.at[:, to : to + 96, my_tile],
            taker[k], near_slot + core, taker_here[k],
        )
    for k, to in enumerate((192, 0)):
        send(
            obj.at[:, 96:288, :], ext.at[:, to : to + 192, my_tile],
            taker[k], far_slot + core, taker_here[k],
        )

    canvas[...] = jnp.zeros_like(canvas)
    canvas_2[...] = jnp.zeros_like(canvas_2)
    result[:, :MARGIN, :] = jnp.zeros((2, MARGIN, WIDE), jnp.float32)
    result[:, MARGIN + PITCH :, :] = jnp.zeros((2, MARGIN, WIDE), jnp.float32)
    for k in range(2):
        arrived(shifts.at[2 * k : 2 * k + 2], shift_slot + k)

    edge = MARGIN + MARGIN * low
    halo = 288 * low
    pair_slot = slots(2)
    from_ext = []
    for k in range(2):
        arrived(ext.at[:, 0:96, tile_lanes(k)], near_slot + k)
        from_ext.append(
            send(
                ext.at[:, rows_from(edge, 96), tile_lanes(k)],
                ext.at[:, rows_from(288 - halo, 96), tile_lanes(k)], pair, pair_slot + k,
            )
        )
    amp_slot = slots(4)
    for j in range(2):
        for k in range(2):
            send(
                amplitudes.at[k * WIN : (k + 1) * WIN, j * WIN : (j + 1) * WIN],
                raw_amps.at[2 * core + j], taker[k], amp_slot + 2 * core + j, taker_here[k],
            )

    loads[0].wait()
    for number in range(4):
        for part in range(2):
            turn = [spread(shifts[number, axis], (WIN, WIN)) for axis in range(2)]
            probes[number, part] = rolled(rolled(probe[part], turn[0], 0), turn[1], 1)
    for load in loads[1:]:
        load.wait()

    own_lanes = ((OWN, 0), (OWN + WIDE - 128, 32))
    margin_lanes = ((0, 32), (OWN + WIDE, 0))

    def send_cols(way, source, lanes, start, depth, sends, recvs, slot):
        pack(source, *lanes[way], start, depth, sends.at[way])
        send(sends.at[way], recvs.at[way], after if way else before, slot + way)

    def place_halo(way, recvs, start, depth, slot):
        arrived(recvs.at[way], slot + way)
        for part in range(2):
            for g in range(4):
                here = rows_from(start + g * depth, depth)
                if way:
                    ext[part, here, :OWN] = unpack(recvs.at[1], 32, depth, part, g, has_before)
                else:
                    ext[part, here, OWN + WIDE :] = unpack(recvs.at[0], 0, depth, part, g, has_after)

    def add_cols(way, target, recvs, slot):
        arrived(recvs.at[way], slot + way)
        for part in range(2):
            for g in range(4):
                here = slice(96 * g, 96 * g + 96)
                if way:
                    target[part, here, lanes_of(0)] += unpack(recvs.at[1], 0, 96, part, g, has_before)
                else:
                    target[part, here, lanes_of(5)] += unpack(recvs.at[0], 32, 96, part, g, has_after)

    first_slot, halo_slot = slots(2), slots(2)
    most = MARGIN - MARGIN * low
    for k in range(2):
        arrived(ext.at[:, 0:192, tile_lanes(k)], far_slot + k)
    for way in (1, 0):
        send_cols(way, ext, own_lanes, most, 72, first_send, first_recv, first_slot)
    for k in range(2):
        arrived(ext.at[:, 0:96, tile_lanes(k)], pair_slot + k)
    here = rows_from(halo, 96)
    ext[:, here, OWN : OWN + WIDE] = jnp.where(has_pair, ext[:, here, OWN : OWN + WIDE], 0.0)
    for way in (1, 0):
        send_cols(way, ext, own_lanes, halo, 24, halo_send, halo_recv, halo_slot)

    def permuted(number):
        arrived(raw_amps.at[number], amp_slot + number)
        pattern = sum(dot(piece, parity[0]) for piece in split(raw_amps[number]))
        amps[number] = sum(dot(parity[1], piece) for piece in split(pattern))

    def gradient(target, number):
        window(ext, target, probes, amps, tables, shifts, number)

    def add_tv(side):
        def step(number, carry):
            start = number * 48
            here = rows_from(MARGIN + start, 48)
            for part, value in enumerate(tv_rows(ext, start, 48, side)):
                canvas[part, here, tile_lanes(side)] += tv_weight * value
            return carry

        lax.fori_loop(0, 4, step, 0)

    row_slot = slots(12)

    def send_block(block):
        lanes = slice(128 * block, 128 * block + 128)
        slot = row_slot + 2 * block
        send(canvas.at[:, :192, lanes_of(block)], rows_recv.at[0, :, :, lanes], above, slot)
        send(canvas.at[:, 192:, lanes_of(block)], rows_recv.at[1, :, :, lanes], below, slot + 1)

    def take_block(block):
        theirs = slice(128 * block, 128 * block + 128)
        for source, keep, starts in ((1, has_above, (0, 96)), (0, has_below, (288, 192))):
            arrived(rows_recv.at[source, :, :, theirs], row_slot + 2 * block + source)
            for start in starts:
                at = start % 192
                for part in range(2):
                    total = canvas[part, start : start + 96, lanes_of(block)] + jnp.where(
                        keep, rows_recv[source, part, at : at + 96, theirs], 0.0
                    )
                    if start in (0, 288):
                        total = jnp.where(keep, total, 0.0)
                    ext[part, start : start + 96, lanes_of(block)] -= step_size * total

    permuted(0)
    place_halo(1, first_recv, most, 72, first_slot)
    place_halo(1, halo_recv, halo, 24, halo_slot)
    gradient(canvas, 0)
    grad_slot = slots(2)
    send_cols(0, canvas, margin_lanes, 0, 96, grad_send, grad_recv, grad_slot)
    permuted(1)
    gradient(canvas, 1)
    place_halo(0, first_recv, most, 72, first_slot)
    place_halo(0, halo_recv, halo, 24, halo_slot)
    add_tv(0)
    send_block(1)
    permuted(2)
    gradient(canvas, 2)
    send_block(2)
    permuted(3)
    gradient(canvas, 3)
    send_cols(1, canvas, margin_lanes, 0, 96, grad_send, grad_recv, grad_slot)
    add_tv(1)
    add_cols(0, canvas, grad_recv, grad_slot)
    send_block(5)
    add_cols(1, canvas, grad_recv, grad_slot)
    send_block(0)
    send_block(3)
    send_block(4)
    next_slot = slots(2)
    for end in from_ext:
        end()
        ends.remove(end)
    take_block(1)
    take_block(2)
    take_block(5)
    send_cols(1, ext, own_lanes, 0, 96, next_send, next_recv, next_slot)
    take_block(0)
    send_cols(0, ext, own_lanes, 0, 96, next_send, next_recv, next_slot)
    place_halo(1, next_recv, 0, 96, next_slot)

    sum_slot, main_slot, rest_slot = slots(6), slots(6), slots(6)

    def start_result(side):
        def step(number, carry):
            start = number * 48
            here = rows_from(MARGIN + start, 48)
            for part, value in enumerate(tv_rows(ext, start, 48, side)):
                cells = ext[part, here, tile_lanes(side)]
                result[part, here, TILE * side : TILE * side + TILE] = (
                    cells - (step_size * tv_weight) * value
                )
            return carry

        lax.fori_loop(0, 4, step, 0)

    def finish(block):
        lanes = slice(128 * block, 128 * block + 128)
        there = slice(128 * (block % 3), 128 * (block % 3) + 128)
        send(
            canvas_2.at[:, rows_from(halo, 96), lanes_of(block)],
            pair_recv.at[:, :, lanes], pair, sum_slot + block,
        )
        result[:, :, lanes] -= step_size * canvas_2[:, :, lanes_of(block)]
        send(
            result.at[:, rows_from(192 - 192 * low, 192), lanes], result_recv.at[low, :, :, there],
            holder[block // 3], main_slot + 2 * (block % 3) + low, holder_here[block // 3],
        )

    def finish_rest(block):
        lanes = slice(128 * block, 128 * block + 128)
        there = slice(128 * (block % 3), 128 * (block % 3) + 128)
        arrived(pair_recv.at[:, :, lanes], sum_slot + block)
        here = rows_from(edge, 96)
        result[:, here, lanes] -= jnp.where(has_pair, step_size * pair_recv[:, :, lanes], 0.0)
        send(
            result.at[:, here, lanes], out.at[:, rows_from(halo, 96), there],
            holder[block // 3], rest_slot + 2 * (block % 3) + low, holder_here[block // 3],
        )

    gradient(canvas_2, 0)
    last_slot = slots(2)
    send_cols(0, canvas_2, margin_lanes, 0, 96, last_send, last_recv, last_slot)
    take_block(3)
    gradient(canvas_2, 1)
    start_result(0)
    finish(1)
    take_block(4)
    gradient(canvas_2, 2)
    finish(2)
    place_halo(0, next_recv, 0, 96, next_slot)
    gradient(canvas_2, 3)
    send_cols(1, canvas_2, margin_lanes, 0, 96, last_send, last_recv, last_slot)
    finish_rest(1)
    start_result(1)
    finish(3)
    finish(4)
    add_cols(0, canvas_2, last_recv, last_slot)
    finish(5)
    add_cols(1, canvas_2, last_recv, last_slot)
    finish(0)
    for block in (2, 3, 4, 5, 0):
        finish_rest(block)
    for block in (1, 2, 0):
        lanes = slice(128 * block, 128 * block + 128)
        for k in range(2):
            arrived(result_recv.at[k, :, :, lanes], main_slot + 2 * block + k)
        out[:, 96:288, lanes] = result_recv[0, :, :, lanes] + result_recv[1, :, :, lanes]
    for block in (1, 2, 0):
        lanes = slice(128 * block, 128 * block + 128)
        for k, start in enumerate((0, 288)):
            arrived(out.at[:, start : start + 96, lanes], rest_slot + 2 * block + k)
    for end in ends:
        end()


def on_device(object_field, probe, amplitudes, offsets):
    vmem = pl.BlockSpec(memory_space=pltpu.VMEM)
    left_there = pl.BlockSpec(memory_space=pl.ANY)

    def pair(depth):
        return [pltpu.VMEM((2, 2, depth, 128), jnp.float32)] * 2

    tables, parity = dft_tables(), parity_table()
    return pl.pallas_call(
        kernel,
        out_shape=jax.ShapeDtypeStruct((2, TILE, TILE), jnp.float32),
        in_specs=[pl.BlockSpec(memory_space=pltpu.SMEM)] + [left_there] * 5,
        out_specs=vmem,
        scratch_shapes=[
            pltpu.VMEM((2, ROWS, COLS), jnp.float32),
            pltpu.VMEM((2, ROWS, COLS), jnp.float32),
            pltpu.VMEM((2, ROWS, COLS), jnp.float32),
            pltpu.VMEM((4, 2, WIN, WIN), jnp.float32),
            pltpu.VMEM((4, WIN, WIN), jnp.float32),
            pltpu.VMEM(probe.shape, jnp.float32),
            pltpu.VMEM(tables.shape, jnp.bfloat16),
            pltpu.VMEM(parity.shape, jnp.bfloat16),
            pltpu.VMEM((2, 2, 2, 8, 128), jnp.int32),
            pltpu.VMEM((4, 2, 8, 128), jnp.int32),
            pltpu.VMEM((4, WIN, WIN), jnp.float32),
            *pair(216), *pair(72),
            *pair(288), *pair(288), *pair(288),
            pltpu.VMEM((2, 2, 192, WIDE), jnp.float32),
            pltpu.VMEM((2, MARGIN, WIDE), jnp.float32),
            pltpu.VMEM((2, ROWS, WIDE), jnp.float32),
            pltpu.VMEM((2, 2, 192, TILE), jnp.float32),
            pltpu.SemaphoreType.DMA((64,)),
            pltpu.SemaphoreType.DMA((64,)),
            pltpu.SemaphoreType.DMA((3,)),
        ],
        compiler_params=pltpu.CompilerParams(
            collective_id=0, has_side_effects=True, vmem_limit_bytes=58 << 20
        ),
        name="ptycho",
    )(offsets, object_field, probe, amplitudes, jnp.asarray(tables), jnp.asarray(parity))


def solution(mesh):
    in_specs = (P(None, "row", "col"), P(), P("row", "col"), P("row", "col", None))
    out_specs = P(None, "row", "col")
    return jax.shard_map(
        on_device, mesh=mesh, in_specs=in_specs, out_specs=out_specs, check_vma=False
    )
```

```python
import functools

import jax
import jax.numpy as jnp
import ml_dtypes
import numpy as np
from jax import lax
from jax.experimental import pallas as pl
from jax.experimental.pallas import tpu as pltpu
from jax.sharding import PartitionSpec as P

WIN = 256
HALF = 128
MARGIN = 96
PITCH = 192
TILE = 384
ROWS = PITCH + 2 * MARGIN
COLS = 1024
OWN = 128
WIDE = 2 * TILE
THIRD = 256
THIRD_LANES = THIRD + 256
BASES = (0, 128, 384, 512)

step_size = 0.3
tv_weight = 0.2
tv_smooth = 0.1
amp_floor = 0.5

MESH = pl.DeviceIdType.MESH


def dft_tables():
    n = np.arange(HALF)
    whole = []
    for odd in (0, 1):
        k = 2 * np.arange(HALF) + odd
        angle = 2.0 * np.pi * ((k[:, None] * n[None, :]) % WIN) / WIN
        cosine = np.cos(angle) / 16.0
        sine = np.sin(angle) / 16.0
        left_form = np.block([[cosine, sine], [-sine, cosine]])
        whole += [left_form, left_form.T]
    high = [m.astype(ml_dtypes.bfloat16) for m in whole]
    low = [(m - h.astype(np.float64)).astype(ml_dtypes.bfloat16) for m, h in zip(whole, high)]
    return np.stack(high + low)


def parity_table():
    table = np.zeros((WIN, WIN), ml_dtypes.bfloat16)
    order = np.concatenate([np.arange(0, WIN, 2), np.arange(1, WIN, 2)])
    table[order, np.arange(WIN)] = 1.0
    return np.stack([table, table.T])


def split(x):
    high = x.astype(jnp.bfloat16)
    return high, (x - high.astype(jnp.float32)).astype(jnp.bfloat16)


def dot(a, b):
    return jnp.dot(a, b, preferred_element_type=jnp.float32)


def cat(a, b, axis):
    return jnp.concatenate([a, b], axis=axis)


def left(tables, k, x):
    high, low = split(x)
    return dot(tables[k], high) + dot(tables[k], low) + dot(tables[k + 4], high)


def right(x, tables, k):
    high, low = split(x)
    return dot(high, tables[k]) + dot(low, tables[k]) + dot(high, tables[k + 4])


def fitted(spectrum, amp):
    re, im = spectrum[:, :HALF], spectrum[:, HALF:]
    magnitude = jnp.sqrt(re * re + im * im)
    keeping = 1.0 - amp / jnp.maximum(magnitude, amp_floor)
    return cat(re * keeping, im * keeping, 1)


def back_field(re, im, amp, tables):
    even = left(tables, 0, cat(re[:HALF] + re[HALF:], im[:HALF] + im[HALF:], 0))
    odd = left(tables, 2, cat(re[:HALF] - re[HALF:], im[:HALF] - im[HALF:], 0))
    re, im = cat(even[:HALF], odd[:HALF], 0), cat(even[HALF:], odd[HALF:], 0)
    even = cat(re[:, :HALF] + re[:, HALF:], im[:, :HALF] + im[:, HALF:], 1)
    odd = cat(re[:, :HALF] - re[:, HALF:], im[:, :HALF] - im[:, HALF:], 1)
    even = fitted(right(even, tables, 1), amp[:, :HALF])
    odd = fitted(right(odd, tables, 3), amp[:, HALF:])
    u, v = right(even, tables, 0), right(odd, tables, 2)
    p, m = u + v, u - v
    re, im = cat(p[:, :HALF], m[:, :HALF], 1), cat(p[:, HALF:], m[:, HALF:], 1)
    u = left(tables, 1, cat(re[:HALF], im[:HALF], 0))
    v = left(tables, 3, cat(re[HALF:], im[HALF:], 0))
    p, m = u + v, u - v
    return cat(p[:HALF], m[:HALF], 0), cat(p[HALF:], m[HALF:], 0)


def spread(plane, shape):
    return jnp.broadcast_to(cat(plane[0:1, :], plane[0:1, :], 1), shape)


def window(ext, canvas, probes, amps, tables, shifts, number):
    first = BASES[number]
    shape = (HALF, WIN)
    by_row = lax.broadcasted_iota(jnp.int32, shape, 0) >= spread(shifts[number, 0], shape)
    by_col = lax.broadcasted_iota(jnp.int32, shape, 1) >= spread(shifts[number, 1], shape)

    def rows_at(part, start):
        near = ext[part, start : start + HALF, first : first + WIN]
        far = ext[part, start : start + HALF, first + WIN : first + 2 * WIN]
        return jnp.where(by_col, near, far)

    def cells(part):
        upper = jnp.where(by_row, rows_at(part, 0), rows_at(part, WIN))
        return cat(upper, rows_at(part, HALF), 0)

    re, im = cells(0), cells(1)
    probe_re, probe_im = probes[number, 0], probes[number, 1]
    back_re, back_im = back_field(
        probe_re * re - probe_im * im, probe_re * im + probe_im * re, amps[number], tables
    )
    grads = (probe_re * back_re + probe_im * back_im, probe_re * back_im - probe_im * back_re)
    for part, grad in enumerate(grads):
        upper, lower = grad[:HALF], grad[HALF:]
        for start, value in (
            (0, jnp.where(by_row, upper, 0.0)),
            (HALF, lower),
            (WIN, jnp.where(by_row, 0.0, upper)),
        ):
            canvas[part, start : start + HALF, first : first + WIN] += jnp.where(by_col, value, 0.0)
            canvas[part, start : start + HALF, first + WIN : first + 2 * WIN] += jnp.where(
                by_col, 0.0, value
            )


def rolled(x, amount, axis):
    for bit in range(8):
        x = jnp.where((amount & (1 << bit)) != 0, pltpu.roll(x, 1 << bit, axis), x)
    return x


def lane_part(depth):
    return lax.broadcasted_iota(jnp.int32, (depth, 128), 1) // 32


def turned(x, amount):
    amount %= 128
    return pltpu.roll(x, amount, 1) if amount else x


def pack(source, lane, skip, start, depth, target):
    part_of = lane_part(depth)
    for part in range(2):
        groups = [
            source[part, pl.ds(pl.multiple_of(start + g * depth, 8), depth), lane : lane + 128]
            for g in range(4)
        ]
        for third in range(3):
            value = turned(groups[0], -32 * third - skip)
            for g in range(1, 4):
                value = jnp.where(part_of == g, turned(groups[g], 32 * (g - third) - skip), value)
            target[part, third * depth : (third + 1) * depth, :] = value


def unpack(source, skip, depth, part, g, keep):
    part_of = lane_part(depth)
    value = jnp.zeros((depth, 128), jnp.float32)
    for third in range(3):
        block = turned(source[part, third * depth : (third + 1) * depth, :], skip + 32 * (third - g))
        value = jnp.where(part_of == third + skip // 32, block, value)
    return jnp.where(keep, value, 0.0)


def tv_rows(ext, start, depth, side):
    high = depth + 16
    first = pl.multiple_of(MARGIN + start - 8, 8)
    lanes = slice(THIRD * side, THIRD * side + THIRD_LANES)
    fields = [ext[part, pl.ds(first, high), lanes] for part in range(2)]
    down = [pltpu.roll(f, high - 1, 0) - f for f in fields]
    right_ = [pltpu.roll(f, THIRD_LANES - 1, 1) - f for f in fields]
    total = down[0] * down[0] + right_[0] * right_[0] + (down[1] * down[1] + right_[1] * right_[1])
    inverse = lax.rsqrt(total + tv_smooth)
    out = []
    for part in range(2):
        flow_down = down[part] * inverse
        flow_right = right_[part] * inverse
        value = pltpu.roll(flow_down, 1, 0) - flow_down + pltpu.roll(flow_right, 1, 1) - flow_right
        out.append(value[8 : depth + 8, OWN : OWN + THIRD])
    return out


def lanes_of(block):
    return slice(OWN + 128 * block, OWN + 128 * block + 128)


def kernel(
    offsets, obj, probe_in, amplitudes, tables_in, parity_in, out,
    ext, canvas, canvas_2, probes, amps, probe, tables, parity,
    planes, shifts, raw_amps,
    first_send, first_recv, halo_send, halo_recv,
    grad_send, grad_recv, next_send, next_recv, last_send, last_recv,
    rows_recv, pair_recv, result, result_recv,
    send_sem, recv_sem, load_sem,
):
    row, col = lax.axis_index("row"), lax.axis_index("col")
    rows, cols = lax.axis_size("row"), lax.axis_size("col")
    quad, low, core = col // 4, lax.rem(col // 2, 2), lax.rem(col, 2)
    quads = cols // 4

    def device(at_row, at_quad, at_low, at_core):
        return (
            lax.rem(at_row + rows, rows),
            4 * lax.rem(at_quad + quads, quads) + 2 * at_low + at_core,
        )

    holder = [device(row, quad, core, k) for k in range(2)]
    holder_here = [(low == core) & (core == k) for k in range(2)]
    taker = [device(row, quad, k, low) for k in range(2)]
    taker_here = [(low == k) & (core == k) for k in range(2)]
    above = device(row - 1 + low, quad, 1 - low, core)
    below = device(row + low, quad, 1 - low, core)
    pair = device(row - 1 + 2 * low, quad, 1 - low, core)
    before = device(row, quad - 1 + core, low, 1 - core)
    after = device(row, quad + core, low, 1 - core)
    across = device(row, quad - 1 + 2 * core, low, 1 - core)
    has_above = (row > 0) | (low > 0)
    has_below = (row < rows - 1) | (low == 0)
    has_pair = ((low == 0) & (row > 0)) | ((low == 1) & (row < rows - 1))
    has_before = (quad > 0) | (core > 0)
    has_after = (quad < quads - 1) | (core == 0)

    loads = [
        pltpu.make_async_copy(source, target, load_sem.at[k])
        for k, (source, target) in enumerate(
            ((probe_in, probe), (parity_in, parity), (tables_in, tables))
        )
    ]
    for load in loads:
        load.start()
    barrier = pltpu.get_barrier_semaphore()
    for other in (
        device(row, quad, low, 1 - core), device(row, quad, 1 - low, core),
        device(row, quad, 1 - low, 1 - core), pair, across,
    ):
        pl.semaphore_signal(barrier, inc=1, device_id=other, device_id_type=MESH)
    pl.semaphore_wait(barrier, 5)

    sent, taken = [0], [0]
    ends = []

    def slots(count):
        taken[0] += count
        return taken[0] - count

    def send(source, target, other, slot, here=None):
        number = sent[0]
        sent[0] += 1
        remote = pltpu.make_async_remote_copy(
            src_ref=source, dst_ref=target, send_sem=send_sem.at[number], recv_sem=recv_sem.at[slot],
            device_id=other, device_id_type=MESH,
        )
        if here is None:
            remote.start()
            ends.append(remote.wait_send)
            return remote.wait_send
        local = pltpu.make_async_copy(source, target, recv_sem.at[slot])
        pl.when(here)(local.start)
        pl.when(jnp.logical_not(here))(remote.start)
        ends.append(lambda: pl.when(jnp.logical_not(here))(remote.wait_send))

    def arrived(target, slot):
        pltpu.make_async_copy(target, target, recv_sem.at[slot]).wait()

    def rows_from(start, depth):
        return pl.ds(pl.multiple_of(start, 8), depth)

    my_tile = pl.ds(pl.multiple_of(OWN + TILE * core, 128), TILE)

    def tile_lanes(k):
        return slice(OWN + TILE * k, OWN + TILE * k + TILE)

    def third_lanes(side):
        return slice(OWN + THIRD * side, OWN + THIRD * side + THIRD)

    for i in range(2):
        for j in range(2):
            planes[i, j, 0] = jnp.full((8, 128), offsets[i, j, 0], jnp.int32)
            planes[i, j, 1] = jnp.full((8, 128), offsets[i, j, 1] + (32 + 64 * j), jnp.int32)
    shift_slot, near_slot, far_slot = slots(2), slots(2), slots(2)
    two = pl.ds(2 * core, 2)
    for k in range(2):
        send(planes.at[k], shifts.at[two], taker[k], shift_slot + core, taker_here[k])
    for k, (start, to) in enumerate(((0, 96), (288, 192))):
        send(
            obj.at[:, start : start + 96, :], ext.at[:, to : to + 96, my_tile],
            taker[k], near_slot + core, taker_here[k],
        )
    inner_slot = slots(2)
    for slot, lane, width in ((far_slot, 256 * core, 128), (inner_slot, 128 - 128 * core, 256)):
        from_lanes = pl.ds(pl.multiple_of(lane, 128), width)
        to_lanes = pl.ds(pl.multiple_of(OWN + TILE * core + lane, 128), width)
        for k, to in enumerate((192, 0)):
            send(
                obj.at[:, 96:288, from_lanes], ext.at[:, to : to + 192, to_lanes],
                taker[k], slot + core, taker_here[k],
            )

    canvas[...] = jnp.zeros_like(canvas)
    canvas_2[...] = jnp.zeros_like(canvas_2)
    result[:, :MARGIN, :] = jnp.zeros((2, MARGIN, WIDE), jnp.float32)
    result[:, MARGIN + PITCH :, :] = jnp.zeros((2, MARGIN, WIDE), jnp.float32)
    for k in range(2):
        arrived(shifts.at[2 * k : 2 * k + 2], shift_slot + k)

    edge = MARGIN + MARGIN * low
    halo = 288 * low
    pair_slot = slots(2)
    from_ext = []
    for k in range(2):
        arrived(ext.at[:, 0:96, tile_lanes(k)], near_slot + k)
        from_ext.append(
            send(
                ext.at[:, rows_from(edge, 96), tile_lanes(k)],
                ext.at[:, rows_from(288 - halo, 96), tile_lanes(k)], pair, pair_slot + k,
            )
        )
    amp_slot = slots(4)
    for j in range(2):
        for k in range(2):
            send(
                amplitudes.at[k * WIN : (k + 1) * WIN, j * WIN : (j + 1) * WIN],
                raw_amps.at[2 * core + j], taker[k], amp_slot + 2 * core + j, taker_here[k],
            )

    loads[0].wait()
    for number in range(4):
        for part in range(2):
            turn = [spread(shifts[number, axis], (WIN, WIN)) for axis in range(2)]
            probes[number, part] = rolled(rolled(probe[part], turn[0], 0), turn[1], 1)
    for load in loads[1:]:
        load.wait()

    own_lanes = ((OWN, 0), (OWN + WIDE - 128, 32))
    margin_lanes = ((0, 32), (OWN + WIDE, 0))

    def send_cols(way, source, lanes, start, depth, sends, recvs, slot):
        pack(source, *lanes[way], start, depth, sends.at[way])
        send(sends.at[way], recvs.at[way], after if way else before, slot + way)

    def place_halo(way, recvs, start, depth, slot):
        arrived(recvs.at[way], slot + way)
        for part in range(2):
            for g in range(4):
                here = rows_from(start + g * depth, depth)
                if way:
                    ext[part, here, :OWN] = unpack(recvs.at[1], 32, depth, part, g, has_before)
                else:
                    ext[part, here, OWN + WIDE :] = unpack(recvs.at[0], 0, depth, part, g, has_after)

    def add_cols(way, target, recvs, slot):
        arrived(recvs.at[way], slot + way)
        for part in range(2):
            for g in range(4):
                here = slice(96 * g, 96 * g + 96)
                if way:
                    target[part, here, lanes_of(0)] += unpack(recvs.at[1], 0, 96, part, g, has_before)
                else:
                    target[part, here, lanes_of(5)] += unpack(recvs.at[0], 32, 96, part, g, has_after)

    first_slot, halo_slot = slots(2), slots(2)
    most = MARGIN - MARGIN * low
    for k in range(2):
        arrived(ext.at[:, 0:192, lanes_of(0)], far_slot + k)
    for way in (1, 0):
        send_cols(way, ext, own_lanes, most, 72, first_send, first_recv, first_slot)
    for k in range(2):
        arrived(ext.at[:, 0:96, tile_lanes(k)], pair_slot + k)
    here = rows_from(halo, 96)
    ext[:, here, OWN : OWN + WIDE] = jnp.where(has_pair, ext[:, here, OWN : OWN + WIDE], 0.0)
    for way in (1, 0):
        send_cols(way, ext, own_lanes, halo, 24, halo_send, halo_recv, halo_slot)
    for k in range(2):
        arrived(ext.at[:, 0:192, 0:256], inner_slot + k)

    def permuted(number):
        arrived(raw_amps.at[number], amp_slot + number)
        pattern = sum(dot(piece, parity[0]) for piece in split(raw_amps[number]))
        amps[number] = sum(dot(parity[1], piece) for piece in split(pattern))

    def gradient(target, number):
        window(ext, target, probes, amps, tables, shifts, number)

    def add_tv(side):
        def step(number, carry):
            start = number * 48
            here = rows_from(MARGIN + start, 48)
            for part, value in enumerate(tv_rows(ext, start, 48, side)):
                canvas[part, here, third_lanes(side)] += tv_weight * value
            return carry

        lax.fori_loop(0, 4, step, 0)

    row_slot = slots(12)

    def send_block(block):
        lanes = slice(128 * block, 128 * block + 128)
        slot = row_slot + 2 * block
        send(canvas.at[:, :192, lanes_of(block)], rows_recv.at[0, :, :, lanes], above, slot)
        send(canvas.at[:, 192:, lanes_of(block)], rows_recv.at[1, :, :, lanes], below, slot + 1)

    def take_block(block):
        theirs = slice(128 * block, 128 * block + 128)
        for source, keep, starts in ((1, has_above, (0, 96)), (0, has_below, (288, 192))):
            arrived(rows_recv.at[source, :, :, theirs], row_slot + 2 * block + source)
            for start in starts:
                at = start % 192
                for part in range(2):
                    total = canvas[part, start : start + 96, lanes_of(block)] + jnp.where(
                        keep, rows_recv[source, part, at : at + 96, theirs], 0.0
                    )
                    if start in (0, 288):
                        total = jnp.where(keep, total, 0.0)
                    ext[part, start : start + 96, lanes_of(block)] -= step_size * total

    permuted(0)
    place_halo(1, first_recv, most, 72, first_slot)
    place_halo(1, halo_recv, halo, 24, halo_slot)
    gradient(canvas, 0)
    grad_slot = slots(2)
    send_cols(0, canvas, margin_lanes, 0, 96, grad_send, grad_recv, grad_slot)
    permuted(1)
    gradient(canvas, 1)
    place_halo(0, first_recv, most, 72, first_slot)
    place_halo(0, halo_recv, halo, 24, halo_slot)
    add_tv(0)
    send_block(1)
    permuted(2)
    gradient(canvas, 2)
    add_tv(1)
    send_block(2)
    permuted(3)
    gradient(canvas, 3)
    send_cols(1, canvas, margin_lanes, 0, 96, grad_send, grad_recv, grad_slot)
    add_tv(2)
    add_cols(0, canvas, grad_recv, grad_slot)
    send_block(5)
    add_cols(1, canvas, grad_recv, grad_slot)
    send_block(0)
    send_block(3)
    send_block(4)
    next_slot = slots(2)
    for end in from_ext:
        end()
        ends.remove(end)
    take_block(1)
    take_block(2)
    take_block(5)
    send_cols(1, ext, own_lanes, 0, 96, next_send, next_recv, next_slot)
    take_block(0)
    send_cols(0, ext, own_lanes, 0, 96, next_send, next_recv, next_slot)
    place_halo(1, next_recv, 0, 96, next_slot)

    sum_slot, main_slot, rest_slot = slots(6), slots(6), slots(6)

    def start_result(side):
        def step(number, carry):
            start = number * 48
            here = rows_from(MARGIN + start, 48)
            for part, value in enumerate(tv_rows(ext, start, 48, side)):
                cells = ext[part, here, third_lanes(side)]
                result[part, here, THIRD * side : THIRD * side + THIRD] = (
                    cells - (step_size * tv_weight) * value
                )
            return carry

        lax.fori_loop(0, 4, step, 0)

    def finish(block):
        lanes = slice(128 * block, 128 * block + 128)
        there = slice(128 * (block % 3), 128 * (block % 3) + 128)
        send(
            canvas_2.at[:, rows_from(halo, 96), lanes_of(block)],
            pair_recv.at[:, :, lanes], pair, sum_slot + block,
        )
        result[:, :, lanes] -= step_size * canvas_2[:, :, lanes_of(block)]
        send(
            result.at[:, rows_from(192 - 192 * low, 192), lanes], result_recv.at[low, :, :, there],
            holder[block // 3], main_slot + 2 * (block % 3) + low, holder_here[block // 3],
        )

    def finish_rest(block):
        lanes = slice(128 * block, 128 * block + 128)
        there = slice(128 * (block % 3), 128 * (block % 3) + 128)
        arrived(pair_recv.at[:, :, lanes], sum_slot + block)
        here = rows_from(edge, 96)
        result[:, here, lanes] -= jnp.where(has_pair, step_size * pair_recv[:, :, lanes], 0.0)
        send(
            result.at[:, here, lanes], out.at[:, rows_from(halo, 96), there],
            holder[block // 3], rest_slot + 2 * (block % 3) + low, holder_here[block // 3],
        )

    gradient(canvas_2, 0)
    last_slot = slots(2)
    send_cols(0, canvas_2, margin_lanes, 0, 96, last_send, last_recv, last_slot)
    start_result(0)
    take_block(3)
    gradient(canvas_2, 1)
    finish(1)
    take_block(4)
    gradient(canvas_2, 2)
    start_result(1)
    finish(2)
    place_halo(0, next_recv, 0, 96, next_slot)
    gradient(canvas_2, 3)
    send_cols(1, canvas_2, margin_lanes, 0, 96, last_send, last_recv, last_slot)
    finish(3)
    finish_rest(1)
    start_result(2)
    finish(4)
    add_cols(0, canvas_2, last_recv, last_slot)
    finish(5)
    add_cols(1, canvas_2, last_recv, last_slot)
    finish(0)
    for block in (2, 3, 4, 5, 0):
        finish_rest(block)
    writes = []
    for block in (1, 2, 0):
        lanes = slice(128 * block, 128 * block + 128)
        for k in range(2):
            arrived(result_recv.at[k, :, :, lanes], main_slot + 2 * block + k)
        result_recv[0, :, :, lanes] += result_recv[1, :, :, lanes]
        writes.append(
            pltpu.make_async_copy(
                result_recv.at[0, :, :, lanes], out.at[:, 96:288, lanes], load_sem.at[block]
            )
        )
        writes[-1].start()
    for block in (1, 2, 0):
        lanes = slice(128 * block, 128 * block + 128)
        for k, start in enumerate((0, 288)):
            arrived(out.at[:, start : start + 96, lanes], rest_slot + 2 * block + k)
    for write in writes:
        write.wait()
    for end in ends:
        end()


def on_device(object_field, probe, amplitudes, offsets):
    left_there = pl.BlockSpec(memory_space=pl.ANY)

    def pair(depth):
        return [pltpu.VMEM((2, 2, depth, 128), jnp.float32)] * 2

    tables, parity = dft_tables(), parity_table()
    return pl.pallas_call(
        kernel,
        out_shape=jax.ShapeDtypeStruct((2, TILE, TILE), jnp.float32),
        in_specs=[pl.BlockSpec(memory_space=pltpu.SMEM)] + [left_there] * 5,
        out_specs=left_there,
        scratch_shapes=[
            pltpu.VMEM((2, ROWS, COLS), jnp.float32),
            pltpu.VMEM((2, ROWS, COLS), jnp.float32),
            pltpu.VMEM((2, ROWS, COLS), jnp.float32),
            pltpu.VMEM((4, 2, WIN, WIN), jnp.float32),
            pltpu.VMEM((4, WIN, WIN), jnp.float32),
            pltpu.VMEM(probe.shape, jnp.float32),
            pltpu.VMEM(tables.shape, jnp.bfloat16),
            pltpu.VMEM(parity.shape, jnp.bfloat16),
            pltpu.VMEM((2, 2, 2, 8, 128), jnp.int32),
            pltpu.VMEM((4, 2, 8, 128), jnp.int32),
            pltpu.VMEM((4, WIN, WIN), jnp.float32),
            *pair(216), *pair(72),
            *pair(288), *pair(288), *pair(288),
            pltpu.VMEM((2, 2, 192, WIDE), jnp.float32),
            pltpu.VMEM((2, MARGIN, WIDE), jnp.float32),
            pltpu.VMEM((2, ROWS, WIDE), jnp.float32),
            pltpu.VMEM((2, 2, 192, TILE), jnp.float32),
            pltpu.SemaphoreType.DMA((64,)),
            pltpu.SemaphoreType.DMA((64,)),
            pltpu.SemaphoreType.DMA((3,)),
        ],
        compiler_params=pltpu.CompilerParams(
            collective_id=0, has_side_effects=True, vmem_limit_bytes=58 << 20
        ),
        name="ptycho",
    )(offsets, object_field, probe, amplitudes, jnp.asarray(tables), jnp.asarray(parity))


def solution(mesh):
    in_specs = (P(None, "row", "col"), P(), P("row", "col"), P("row", "col", None))
    out_specs = P(None, "row", "col")
    return jax.shard_map(
        on_device, mesh=mesh, in_specs=in_specs, out_specs=out_specs, check_vma=False
    )
```

```python
import functools

import jax
import jax.numpy as jnp
import ml_dtypes
import numpy as np
from jax import lax
from jax.experimental import pallas as pl
from jax.experimental.pallas import tpu as pltpu
from jax.sharding import PartitionSpec as P

WIN = 256
HALF = 128
MARGIN = 96
PITCH = 192
TILE = 384
ROWS = PITCH + 2 * MARGIN
COLS = 1024
OWN = 128
WIDE = 2 * TILE
THIRD = 256
THIRD_LANES = THIRD + 256
BASES = (0, 128, 384, 512)

step_size = 0.3
tv_weight = 0.2
tv_smooth = 0.1
amp_floor = 0.5

MESH = pl.DeviceIdType.MESH


def dft_tables():
    n = np.arange(HALF)
    whole = []
    for odd in (0, 1):
        k = 2 * np.arange(HALF) + odd
        angle = 2.0 * np.pi * ((k[:, None] * n[None, :]) % WIN) / WIN
        cosine = np.cos(angle) / 16.0
        sine = np.sin(angle) / 16.0
        left_form = np.block([[cosine, sine], [-sine, cosine]])
        whole += [left_form, left_form.T]
    high = [m.astype(ml_dtypes.bfloat16) for m in whole]
    low = [(m - h.astype(np.float64)).astype(ml_dtypes.bfloat16) for m, h in zip(whole, high)]
    return np.stack(high + low)


def parity_table():
    table = np.zeros((WIN, WIN), ml_dtypes.bfloat16)
    order = np.concatenate([np.arange(0, WIN, 2), np.arange(1, WIN, 2)])
    table[order, np.arange(WIN)] = 1.0
    return np.stack([table, table.T])


def split(x):
    high = x.astype(jnp.bfloat16)
    return high, (x - high.astype(jnp.float32)).astype(jnp.bfloat16)


def dot(a, b):
    return jnp.dot(a, b, preferred_element_type=jnp.float32)


def cat(a, b, axis):
    return jnp.concatenate([a, b], axis=axis)


def left(tables, k, x):
    high, low = split(x)
    return dot(tables[k], high) + dot(tables[k], low) + dot(tables[k + 4], high)


def right(x, tables, k):
    high, low = split(x)
    return dot(high, tables[k]) + dot(low, tables[k]) + dot(high, tables[k + 4])


def fitted(spectrum, amp):
    re, im = spectrum[:, :HALF], spectrum[:, HALF:]
    magnitude = jnp.sqrt(re * re + im * im)
    keeping = 1.0 - amp / jnp.maximum(magnitude, amp_floor)
    return cat(re * keeping, im * keeping, 1)


def back_field(re, im, amp, tables):
    even = left(tables, 0, cat(re[:HALF] + re[HALF:], im[:HALF] + im[HALF:], 0))
    odd = left(tables, 2, cat(re[:HALF] - re[HALF:], im[:HALF] - im[HALF:], 0))
    re, im = cat(even[:HALF], odd[:HALF], 0), cat(even[HALF:], odd[HALF:], 0)
    even = cat(re[:, :HALF] + re[:, HALF:], im[:, :HALF] + im[:, HALF:], 1)
    odd = cat(re[:, :HALF] - re[:, HALF:], im[:, :HALF] - im[:, HALF:], 1)
    even = fitted(right(even, tables, 1), amp[:, :HALF])
    odd = fitted(right(odd, tables, 3), amp[:, HALF:])
    u, v = right(even, tables, 0), right(odd, tables, 2)
    p, m = u + v, u - v
    re, im = cat(p[:, :HALF], m[:, :HALF], 1), cat(p[:, HALF:], m[:, HALF:], 1)
    u = left(tables, 1, cat(re[:HALF], im[:HALF], 0))
    v = left(tables, 3, cat(re[HALF:], im[HALF:], 0))
    p, m = u + v, u - v
    return cat(p[:HALF], m[:HALF], 0), cat(p[HALF:], m[HALF:], 0)


def spread(plane, shape):
    return jnp.broadcast_to(cat(plane[0:1, :], plane[0:1, :], 1), shape)


def window(ext, canvas, probes, amps, tables, shifts, number):
    first = BASES[number]
    shape = (HALF, WIN)
    by_row = lax.broadcasted_iota(jnp.int32, shape, 0) >= spread(shifts[number, 0], shape)
    by_col = lax.broadcasted_iota(jnp.int32, shape, 1) >= spread(shifts[number, 1], shape)

    def rows_at(part, start):
        near = ext[part, start : start + HALF, first : first + WIN]
        far = ext[part, start : start + HALF, first + WIN : first + 2 * WIN]
        return jnp.where(by_col, near, far)

    def cells(part):
        upper = jnp.where(by_row, rows_at(part, 0), rows_at(part, WIN))
        return cat(upper, rows_at(part, HALF), 0)

    re, im = cells(0), cells(1)
    probe_re, probe_im = probes[number, 0], probes[number, 1]
    back_re, back_im = back_field(
        probe_re * re - probe_im * im, probe_re * im + probe_im * re, amps[number], tables
    )
    grads = (probe_re * back_re + probe_im * back_im, probe_re * back_im - probe_im * back_re)
    for part, grad in enumerate(grads):
        upper, lower = grad[:HALF], grad[HALF:]
        for start, value in (
            (0, jnp.where(by_row, upper, 0.0)),
            (HALF, lower),
            (WIN, jnp.where(by_row, 0.0, upper)),
        ):
            canvas[part, start : start + HALF, first : first + WIN] += jnp.where(by_col, value, 0.0)
            canvas[part, start : start + HALF, first + WIN : first + 2 * WIN] += jnp.where(
                by_col, 0.0, value
            )


def rolled(x, amount, axis):
    for bit in range(8):
        x = jnp.where((amount & (1 << bit)) != 0, pltpu.roll(x, 1 << bit, axis), x)
    return x


def lane_part(depth):
    return lax.broadcasted_iota(jnp.int32, (depth, 128), 1) // 32


def turned(x, amount):
    amount %= 128
    return pltpu.roll(x, amount, 1) if amount else x


def pack(source, lane, skip, start, depth, target):
    part_of = lane_part(depth)
    for part in range(2):
        groups = [
            source[part, pl.ds(pl.multiple_of(start + g * depth, 8), depth), lane : lane + 128]
            for g in range(4)
        ]
        for third in range(3):
            value = turned(groups[0], -32 * third - skip)
            for g in range(1, 4):
                value = jnp.where(part_of == g, turned(groups[g], 32 * (g - third) - skip), value)
            target[part, third * depth : (third + 1) * depth, :] = value


def unpack(source, skip, depth, part, g, keep):
    part_of = lane_part(depth)
    value = jnp.zeros((depth, 128), jnp.float32)
    for third in range(3):
        block = turned(source[part, third * depth : (third + 1) * depth, :], skip + 32 * (third - g))
        value = jnp.where(part_of == third + skip // 32, block, value)
    return jnp.where(keep, value, 0.0)


def tv_rows(ext, start, depth, side):
    high = depth + 16
    first = pl.multiple_of(MARGIN + start - 8, 8)
    lanes = slice(THIRD * side, THIRD * side + THIRD_LANES)
    fields = [ext[part, pl.ds(first, high), lanes] for part in range(2)]
    down = [pltpu.roll(f, high - 1, 0) - f for f in fields]
    right_ = [pltpu.roll(f, THIRD_LANES - 1, 1) - f for f in fields]
    total = down[0] * down[0] + right_[0] * right_[0] + (down[1] * down[1] + right_[1] * right_[1])
    inverse = lax.rsqrt(total + tv_smooth)
    out = []
    for part in range(2):
        flow_down = down[part] * inverse
        flow_right = right_[part] * inverse
        value = pltpu.roll(flow_down, 1, 0) - flow_down + pltpu.roll(flow_right, 1, 1) - flow_right
        out.append(value[8 : depth + 8, OWN : OWN + THIRD])
    return out


def lanes_of(block):
    return slice(OWN + 128 * block, OWN + 128 * block + 128)


def kernel(
    offsets, obj, probe_in, amplitudes, tables_in, parity_in, out,
    ext, canvas, canvas_2, probes, amps, probe, tables, parity,
    planes, shifts, raw_amps,
    first_send, first_recv, halo_send, halo_recv,
    grad_send, grad_recv, next_send, next_recv, last_send, last_recv,
    rows_recv, pair_recv, result, result_recv,
    send_sem, recv_sem, load_sem,
):
    row, col = lax.axis_index("row"), lax.axis_index("col")
    rows, cols = lax.axis_size("row"), lax.axis_size("col")
    quad, low, core = col // 4, lax.rem(col // 2, 2), lax.rem(col, 2)
    quads = cols // 4

    def device(at_row, at_quad, at_low, at_core):
        return (
            lax.rem(at_row + rows, rows),
            4 * lax.rem(at_quad + quads, quads) + 2 * at_low + at_core,
        )

    holder = [device(row, quad, core, k) for k in range(2)]
    holder_here = [(low == core) & (core == k) for k in range(2)]
    taker = [device(row, quad, k, low) for k in range(2)]
    taker_here = [(low == k) & (core == k) for k in range(2)]
    above = device(row - 1 + low, quad, 1 - low, core)
    below = device(row + low, quad, 1 - low, core)
    pair = device(row - 1 + 2 * low, quad, 1 - low, core)
    before = device(row, quad - 1 + core, low, 1 - core)
    after = device(row, quad + core, low, 1 - core)
    across = device(row, quad - 1 + 2 * core, low, 1 - core)
    has_above = (row > 0) | (low > 0)
    has_below = (row < rows - 1) | (low == 0)
    has_pair = ((low == 0) & (row > 0)) | ((low == 1) & (row < rows - 1))
    has_before = (quad > 0) | (core > 0)
    has_after = (quad < quads - 1) | (core == 0)

    loads = [
        pltpu.make_async_copy(source, target, load_sem.at[k])
        for k, (source, target) in enumerate(
            ((probe_in, probe), (parity_in, parity), (tables_in, tables))
        )
    ]
    for load in loads:
        load.start()
    barrier = pltpu.get_barrier_semaphore()
    for other in (
        device(row, quad, low, 1 - core), device(row, quad, 1 - low, core),
        device(row, quad, 1 - low, 1 - core), pair, across,
    ):
        pl.semaphore_signal(barrier, inc=1, device_id=other, device_id_type=MESH)
    pl.semaphore_wait(barrier, 5)

    sent, taken = [0], [0]
    ends = []

    def slots(count):
        taken[0] += count
        return taken[0] - count

    def send(source, target, other, slot, here=None):
        number = sent[0]
        sent[0] += 1
        remote = pltpu.make_async_remote_copy(
            src_ref=source, dst_ref=target, send_sem=send_sem.at[number], recv_sem=recv_sem.at[slot],
            device_id=other, device_id_type=MESH,
        )
        if here is None:
            remote.start()
            ends.append(remote.wait_send)
            return remote.wait_send
        local = pltpu.make_async_copy(source, target, recv_sem.at[slot])
        pl.when(here)(local.start)
        pl.when(jnp.logical_not(here))(remote.start)
        ends.append(lambda: pl.when(jnp.logical_not(here))(remote.wait_send))

    def arrived(target, slot):
        pltpu.make_async_copy(target, target, recv_sem.at[slot]).wait()

    def rows_from(start, depth):
        return pl.ds(pl.multiple_of(start, 8), depth)

    my_tile = pl.ds(pl.multiple_of(OWN + TILE * core, 128), TILE)

    def tile_lanes(k):
        return slice(OWN + TILE * k, OWN + TILE * k + TILE)

    def third_lanes(side):
        return slice(OWN + THIRD * side, OWN + THIRD * side + THIRD)

    for i in range(2):
        for j in range(2):
            planes[i, j, 0] = jnp.full((8, 128), offsets[i, j, 0], jnp.int32)
            planes[i, j, 1] = jnp.full((8, 128), offsets[i, j, 1] + (32 + 64 * j), jnp.int32)
    shift_slot, near_slot, far_slot = slots(2), slots(2), slots(2)
    two = pl.ds(2 * core, 2)
    for k in range(2):
        send(planes.at[k], shifts.at[two], taker[k], shift_slot + core, taker_here[k])
    for k, (start, to) in enumerate(((0, 96), (288, 192))):
        send(
            obj.at[:, start : start + 96, :], ext.at[:, to : to + 96, my_tile],
            taker[k], near_slot + core, taker_here[k],
        )
    inner_slot = slots(2)

    def send_between(slot, lane, width):
        from_lanes = pl.ds(pl.multiple_of(lane, 128), width)
        to_lanes = pl.ds(pl.multiple_of(OWN + TILE * core + lane, 128), width)
        for k, to in enumerate((192, 0)):
            send(
                obj.at[:, 96:288, from_lanes], ext.at[:, to : to + 192, to_lanes],
                taker[k], slot + core, taker_here[k],
            )

    send_between(far_slot, 256 * core, 128)
    canvas[...] = jnp.zeros_like(canvas)
    canvas_2[...] = jnp.zeros_like(canvas_2)
    result[:, :MARGIN, :] = jnp.zeros((2, MARGIN, WIDE), jnp.float32)
    result[:, MARGIN + PITCH :, :] = jnp.zeros((2, MARGIN, WIDE), jnp.float32)
    for k in range(2):
        arrived(shifts.at[2 * k : 2 * k + 2], shift_slot + k)

    edge = MARGIN + MARGIN * low
    halo = 288 * low
    pair_slot = slots(2)
    from_ext = []
    for k in range(2):
        arrived(ext.at[:, 0:96, tile_lanes(k)], near_slot + k)
        from_ext.append(
            send(
                ext.at[:, rows_from(edge, 96), tile_lanes(k)],
                ext.at[:, rows_from(288 - halo, 96), tile_lanes(k)], pair, pair_slot + k,
            )
        )
    send_between(inner_slot, 128 - 128 * core, 256)
    amp_slot = slots(4)
    for j in range(2):
        for k in range(2):
            send(
                amplitudes.at[k * WIN : (k + 1) * WIN, j * WIN : (j + 1) * WIN],
                raw_amps.at[2 * core + j], taker[k], amp_slot + 2 * core + j, taker_here[k],
            )

    loads[0].wait()
    for number in range(4):
        for part in range(2):
            turn = [spread(shifts[number, axis], (WIN, WIN)) for axis in range(2)]
            probes[number, part] = rolled(rolled(probe[part], turn[0], 0), turn[1], 1)
    for load in loads[1:]:
        load.wait()

    own_lanes = ((OWN, 0), (OWN + WIDE - 128, 32))
    margin_lanes = ((0, 32), (OWN + WIDE, 0))

    def send_cols(way, source, lanes, start, depth, sends, recvs, slot):
        pack(source, *lanes[way], start, depth, sends.at[way])
        send(sends.at[way], recvs.at[way], after if way else before, slot + way)

    def place_halo(way, recvs, start, depth, slot):
        arrived(recvs.at[way], slot + way)
        for part in range(2):
            for g in range(4):
                here = rows_from(start + g * depth, depth)
                if way:
                    ext[part, here, :OWN] = unpack(recvs.at[1], 32, depth, part, g, has_before)
                else:
                    ext[part, here, OWN + WIDE :] = unpack(recvs.at[0], 0, depth, part, g, has_after)

    def add_cols(way, target, recvs, slot):
        arrived(recvs.at[way], slot + way)
        for part in range(2):
            for g in range(4):
                here = slice(96 * g, 96 * g + 96)
                if way:
                    target[part, here, lanes_of(0)] += unpack(recvs.at[1], 0, 96, part, g, has_before)
                else:
                    target[part, here, lanes_of(5)] += unpack(recvs.at[0], 32, 96, part, g, has_after)

    first_slot, halo_slot = slots(2), slots(2)
    most = MARGIN - MARGIN * low
    for k in range(2):
        arrived(ext.at[:, 0:192, lanes_of(0)], far_slot + k)
    for way in (1, 0):
        send_cols(way, ext, own_lanes, most, 72, first_send, first_recv, first_slot)
    for k in range(2):
        arrived(ext.at[:, 0:96, tile_lanes(k)], pair_slot + k)
    here = rows_from(halo, 96)
    ext[:, here, OWN : OWN + WIDE] = jnp.where(has_pair, ext[:, here, OWN : OWN + WIDE], 0.0)
    for way in (1, 0):
        send_cols(way, ext, own_lanes, halo, 24, halo_send, halo_recv, halo_slot)
    for k in range(2):
        arrived(ext.at[:, 0:192, 0:256], inner_slot + k)

    def permuted(number):
        arrived(raw_amps.at[number], amp_slot + number)
        pattern = sum(dot(piece, parity[0]) for piece in split(raw_amps[number]))
        amps[number] = sum(dot(parity[1], piece) for piece in split(pattern))

    def gradient(target, number):
        window(ext, target, probes, amps, tables, shifts, number)

    def add_tv(side):
        def step(number, carry):
            start = number * 48
            here = rows_from(MARGIN + start, 48)
            for part, value in enumerate(tv_rows(ext, start, 48, side)):
                canvas[part, here, third_lanes(side)] += tv_weight * value
            return carry

        lax.fori_loop(0, 4, step, 0)

    row_slot = slots(12)

    def send_block(block):
        lanes = slice(128 * block, 128 * block + 128)
        slot = row_slot + 2 * block
        send(canvas.at[:, :192, lanes_of(block)], rows_recv.at[0, :, :, lanes], above, slot)
        send(canvas.at[:, 192:, lanes_of(block)], rows_recv.at[1, :, :, lanes], below, slot + 1)

    def take_block(block):
        theirs = slice(128 * block, 128 * block + 128)
        for source, keep, starts in ((1, has_above, (0, 96)), (0, has_below, (288, 192))):
            arrived(rows_recv.at[source, :, :, theirs], row_slot + 2 * block + source)
            for start in starts:
                at = start % 192
                for part in range(2):
                    total = canvas[part, start : start + 96, lanes_of(block)] + jnp.where(
                        keep, rows_recv[source, part, at : at + 96, theirs], 0.0
                    )
                    if start in (0, 288):
                        total = jnp.where(keep, total, 0.0)
                    ext[part, start : start + 96, lanes_of(block)] -= step_size * total

    permuted(0)
    place_halo(1, first_recv, most, 72, first_slot)
    place_halo(1, halo_recv, halo, 24, halo_slot)
    gradient(canvas, 0)
    grad_slot = slots(2)
    send_cols(0, canvas, margin_lanes, 0, 96, grad_send, grad_recv, grad_slot)
    permuted(1)
    gradient(canvas, 1)
    place_halo(0, first_recv, most, 72, first_slot)
    place_halo(0, halo_recv, halo, 24, halo_slot)
    add_tv(0)
    send_block(1)
    permuted(2)
    gradient(canvas, 2)
    add_tv(1)
    send_block(2)
    permuted(3)
    gradient(canvas, 3)
    send_cols(1, canvas, margin_lanes, 0, 96, grad_send, grad_recv, grad_slot)
    add_tv(2)
    add_cols(0, canvas, grad_recv, grad_slot)
    send_block(5)
    add_cols(1, canvas, grad_recv, grad_slot)
    send_block(0)
    next_slot = slots(2)
    for end in from_ext:
        end()
        ends.remove(end)
    take_block(1)
    take_block(2)
    send_block(3)
    take_block(5)
    send_block(4)
    send_cols(1, ext, own_lanes, 0, 96, next_send, next_recv, next_slot)
    take_block(0)
    send_cols(0, ext, own_lanes, 0, 96, next_send, next_recv, next_slot)
    place_halo(1, next_recv, 0, 96, next_slot)

    sum_slot, main_slot, rest_slot = slots(6), slots(6), slots(6)

    def start_result(side):
        def step(number, carry):
            start = number * 48
            here = rows_from(MARGIN + start, 48)
            for part, value in enumerate(tv_rows(ext, start, 48, side)):
                cells = ext[part, here, third_lanes(side)]
                result[part, here, THIRD * side : THIRD * side + THIRD] = (
                    cells - (step_size * tv_weight) * value
                )
            return carry

        lax.fori_loop(0, 4, step, 0)

    def finish(block):
        lanes = slice(128 * block, 128 * block + 128)
        there = slice(128 * (block % 3), 128 * (block % 3) + 128)
        send(
            canvas_2.at[:, rows_from(halo, 96), lanes_of(block)],
            pair_recv.at[:, :, lanes], pair, sum_slot + block,
        )
        result[:, :, lanes] -= step_size * canvas_2[:, :, lanes_of(block)]
        send(
            result.at[:, rows_from(192 - 192 * low, 192), lanes], result_recv.at[low, :, :, there],
            holder[block // 3], main_slot + 2 * (block % 3) + low, holder_here[block // 3],
        )

    def finish_rest(block):
        lanes = slice(128 * block, 128 * block + 128)
        there = slice(128 * (block % 3), 128 * (block % 3) + 128)
        arrived(pair_recv.at[:, :, lanes], sum_slot + block)
        here = rows_from(edge, 96)
        result[:, here, lanes] -= jnp.where(has_pair, step_size * pair_recv[:, :, lanes], 0.0)
        send(
            result.at[:, here, lanes], out.at[:, rows_from(halo, 96), there],
            holder[block // 3], rest_slot + 2 * (block % 3) + low, holder_here[block // 3],
        )

    gradient(canvas_2, 0)
    last_slot = slots(2)
    send_cols(0, canvas_2, margin_lanes, 0, 96, last_send, last_recv, last_slot)
    start_result(0)
    take_block(3)
    gradient(canvas_2, 1)
    finish(1)
    take_block(4)
    gradient(canvas_2, 2)
    start_result(1)
    finish(2)
    place_halo(0, next_recv, 0, 96, next_slot)
    gradient(canvas_2, 3)
    send_cols(1, canvas_2, margin_lanes, 0, 96, last_send, last_recv, last_slot)
    finish(3)
    finish_rest(1)
    start_result(2)
    finish(4)
    add_cols(0, canvas_2, last_recv, last_slot)
    finish(5)
    add_cols(1, canvas_2, last_recv, last_slot)
    finish(0)
    for block in (2, 3, 4, 5, 0):
        finish_rest(block)
    writes = []
    for block in (1, 2, 0):
        lanes = slice(128 * block, 128 * block + 128)
        for k in range(2):
            arrived(result_recv.at[k, :, :, lanes], main_slot + 2 * block + k)
        result_recv[0, :, :, lanes] += result_recv[1, :, :, lanes]
        writes.append(
            pltpu.make_async_copy(
                result_recv.at[0, :, :, lanes], out.at[:, 96:288, lanes], load_sem.at[block]
            )
        )
        writes[-1].start()
    for block in (1, 2, 0):
        lanes = slice(128 * block, 128 * block + 128)
        for k, start in enumerate((0, 288)):
            arrived(out.at[:, start : start + 96, lanes], rest_slot + 2 * block + k)
    for write in writes:
        write.wait()
    for end in ends:
        end()


def on_device(object_field, probe, amplitudes, offsets):
    left_there = pl.BlockSpec(memory_space=pl.ANY)

    def pair(depth):
        return [pltpu.VMEM((2, 2, depth, 128), jnp.float32)] * 2

    tables, parity = dft_tables(), parity_table()
    return pl.pallas_call(
        kernel,
        out_shape=jax.ShapeDtypeStruct((2, TILE, TILE), jnp.float32),
        in_specs=[pl.BlockSpec(memory_space=pltpu.SMEM)] + [left_there] * 5,
        out_specs=left_there,
        scratch_shapes=[
            pltpu.VMEM((2, ROWS, COLS), jnp.float32),
            pltpu.VMEM((2, ROWS, COLS), jnp.float32),
            pltpu.VMEM((2, ROWS, COLS), jnp.float32),
            pltpu.VMEM((4, 2, WIN, WIN), jnp.float32),
            pltpu.VMEM((4, WIN, WIN), jnp.float32),
            pltpu.VMEM(probe.shape, jnp.float32),
            pltpu.VMEM(tables.shape, jnp.bfloat16),
            pltpu.VMEM(parity.shape, jnp.bfloat16),
            pltpu.VMEM((2, 2, 2, 8, 128), jnp.int32),
            pltpu.VMEM((4, 2, 8, 128), jnp.int32),
            pltpu.VMEM((4, WIN, WIN), jnp.float32),
            *pair(216), *pair(72),
            *pair(288), *pair(288), *pair(288),
            pltpu.VMEM((2, 2, 192, WIDE), jnp.float32),
            pltpu.VMEM((2, MARGIN, WIDE), jnp.float32),
            pltpu.VMEM((2, ROWS, WIDE), jnp.float32),
            pltpu.VMEM((2, 2, 192, TILE), jnp.float32),
            pltpu.SemaphoreType.DMA((64,)),
            pltpu.SemaphoreType.DMA((64,)),
            pltpu.SemaphoreType.DMA((3,)),
        ],
        compiler_params=pltpu.CompilerParams(
            collective_id=0, has_side_effects=True, vmem_limit_bytes=58 << 20
        ),
        name="ptycho",
    )(offsets, object_field, probe, amplitudes, jnp.asarray(tables), jnp.asarray(parity))


def solution(mesh):
    in_specs = (P(None, "row", "col"), P(), P("row", "col"), P("row", "col", None))
    out_specs = P(None, "row", "col")
    return jax.shard_map(
        on_device, mesh=mesh, in_specs=in_specs, out_specs=out_specs, check_vma=False
    )
```
